32 devices in a mesh: band: 2 (over x), img: 4 (over z), fsdp: 4 (over y, core).
Axes of the slice: x: 2, y: 2, z: 4, core: 2. Of those that a mesh axis runs over, the one named last changes fastest.
Arguments:
- block_input: bfloat16 [384, 14, 14, 512], P(('img', 'fsdp'), 'band'), may hold values from -6 to 6
- slot_used: int32 [16, 24], P(('img', 'fsdp')), may hold values from 0 to 1, as said below
- cotangent: bfloat16 [384, 14, 14, 512], P(('img', 'fsdp'), 'band'), may hold values from -6 to 6
- ln1_gain: bfloat16 [512], P('fsdp'), may hold values from 0.25 to 1.75
- ln1_bias: bfloat16 [512], P('fsdp'), may hold values from -3 to 3
- w_qkv: bfloat16 [512, 1536], P('fsdp')
- q_bias: bfloat16 [512], P('fsdp'), may hold values from -3 to 3
- v_bias: bfloat16 [512], P('fsdp'), may hold values from -3 to 3
- rel_table: bfloat16 [16, 169], P('fsdp'), may hold values from -4 to 4
- w_out: bfloat16 [512, 512], P('fsdp'), may hold values from -0.75 to 0.75
- out_bias: bfloat16 [512], P('fsdp'), may hold values from -3 to 3
- ln2_gain: bfloat16 [512], P('fsdp'), may hold values from 0.25 to 1.75
- ln2_bias: bfloat16 [512], P('fsdp'), may hold values from -3 to 3
- w_fc1: bfloat16 [512, 2048], P('fsdp'), may hold values from -0.25 to 0.25
- fc1_bias: bfloat16 [2048], P('fsdp'), may hold values from -3 to 3
- w_fc2: bfloat16 [2048, 512], P('fsdp'), may hold values from -0.125 to 0.125
- fc2_bias: bfloat16 [512], P('fsdp'), may hold values from -3 to 3
Outputs:
- block_output: bfloat16 [384, 14, 14, 512], P(('img', 'fsdp'), 'band')
- input_grad: float32 [384, 14, 14, 512], P(('img', 'fsdp'), 'band')
- ln1_gain_grad: float32 [512], P('fsdp')
- ln1_bias_grad: float32 [512], P('fsdp')
- w_qkv_grad: float32 [512, 1536], P('fsdp')
- q_bias_grad: float32 [512], P('fsdp')
- v_bias_grad: float32 [512], P('fsdp')
- rel_table_grad: float32 [16, 169], P('fsdp')
- w_out_grad: float32 [512, 512], P('fsdp')
- out_bias_grad: float32 [512], P('fsdp')
- ln2_gain_grad: float32 [512], P('fsdp')
- ln2_bias_grad: float32 [512], P('fsdp')
- w_fc1_grad: float32 [512, 2048], P('fsdp')
- fc1_bias_grad: float32 [2048], P('fsdp')
- w_fc2_grad: float32 [2048, 512], P('fsdp')
- fc2_bias_grad: float32 [512], P('fsdp')
The draws below stay inside these ranges and needn't reach their ends.
Inputs may be any that keep to these rules, and one draw needn't show every extreme that they name: `slot_used`: each row holds between 16 and 24 ones in any positions; both counts occur in every draw.
All inputs are finite; a program needn't handle non-finite values.
Results may differ from the reference program's by a relative error of at most 0.013.
The reference program's roundings to bfloat16 on the way count: a program that leaves them out, or rounds other values in their place, can miss the bound.
Values may be sent and summed in bfloat16 or wider, within the bound.
No kernel may reach another device: no remote copies, remote signals or barrier semaphores. Data moves between devices by JAX's collectives and lax.ppermute only.
A program may use at most 320 MiB of HBM per device.

```python
import jax
import jax.numpy as jnp
from jax import lax

D = 512
HEADS = 16
FF = 2048
WIN = 7
SHIFT = 3
SIDE = 14
TABLE = 169
SLOTS = 24
GROUPS = 16
IMAGES = 384


def draw_slot_used(key, part):
    lowest = 2 * SLOTS // 3
    key_count, key_pick, key_order = jax.random.split(key, 3)
    counts = jax.random.randint(key_count, (GROUPS,), lowest, SLOTS + 1)
    chosen = jax.random.randint(key_pick, (), 0, GROUPS)
    places = jnp.arange(GROUPS)
    counts = jnp.where(places == chosen, SLOTS, counts)
    counts = jnp.where(places == (chosen + 1) % GROUPS, lowest, counts)
    orders = jax.vmap(lambda single: jax.random.permutation(single, SLOTS))(jax.random.split(key_order, GROUPS))
    return (orders < counts[:, None]).astype(jnp.int32)


def draw_w_qkv(key, part):
    base = jax.random.normal(jax.random.fold_in(key, 11), (D, 3 * D), jnp.float32) * D ** (-0.5)
    return base.astype(jnp.bfloat16)


def block_levels(own_key, shape, cuts, smallest, largest):
    level, own = 1.0, jax.random.fold_in(own_key, 6)
    for position, blocks in cuts:
        steps = jnp.exp(jax.random.uniform(jax.random.fold_in(own, position), (blocks,), jnp.float32, smallest / len(cuts), largest / len(cuts)))
        level = level * jnp.repeat(steps, shape[position] // blocks).reshape([-1 if axis == position else 1 for axis in range(len(shape))])
    return level


def bell_draw(rng, dims, scale, reach, pieces=(), dtype=jnp.bfloat16):
    result = scale * jax.random.normal(rng, dims, jnp.float32)
    if pieces:
        result = result * block_levels(rng, dims, pieces, -0.22, 0.18)
    return jnp.clip(result, -reach, reach).astype(dtype)


def setup_inputs(seed: int = 0) -> dict:
    streams_of = jax.random.split(jax.random.key(seed), 18)
    block_input = bell_draw(streams_of[0], (IMAGES, SIDE, SIDE, D), 1.0, 6.0, ((0, 16), (1, 2)))
    slot_used = draw_slot_used(jax.random.fold_in(streams_of[17], 71), 0)
    cotangent = bell_draw(streams_of[2], (IMAGES, SIDE, SIDE, D), 1.0, 6.0, ((0, 16), (1, 2)))
    ln1_gain = jnp.clip(1.0 + 0.15 * jax.random.normal(streams_of[3], (D,), jnp.float32), 0.25, 1.75).astype(jnp.bfloat16)
    ln1_bias = bell_draw(streams_of[4], (D,), 0.5, 3.0, ((0, 4),))
    w_qkv = draw_w_qkv(jax.random.fold_in(streams_of[17], 71), 0)
    q_bias = bell_draw(streams_of[6], (D,), 0.5, 3.0, ((0, 4),))
    v_bias = bell_draw(streams_of[7], (D,), 0.5, 3.0, ((0, 4),))
    rel_table = bell_draw(streams_of[8], (HEADS, TABLE), 1.0, 4.0, ((0, 4),))
    w_out = bell_draw(streams_of[9], (D, D), (D // 7) ** -0.5, 0.75, ((0, 4),))
    out_bias = bell_draw(streams_of[10], (D,), 0.5, 3.0, ((0, 4),))
    ln2_gain = jnp.clip(1.0 + 0.15 * jax.random.normal(streams_of[11], (D,), jnp.float32), 0.25, 1.75).astype(jnp.bfloat16)
    ln2_bias = bell_draw(streams_of[12], (D,), 0.5, 3.0, ((0, 4),))
    w_fc1 = bell_draw(streams_of[13], (D, FF), D ** -0.5, 0.25, ((0, 4),))
    fc1_bias = bell_draw(streams_of[14], (FF,), 0.5, 3.0, ((0, 4),))
    w_fc2 = bell_draw(streams_of[15], (FF, D), FF ** -0.5, 0.125, ((0, 4),))
    fc2_bias = bell_draw(streams_of[16], (D,), 0.5, 3.0, ((0, 4),))
    return {"block_input": block_input, "slot_used": slot_used, "cotangent": cotangent, "ln1_gain": ln1_gain, "ln1_bias": ln1_bias, "w_qkv": w_qkv, "q_bias": q_bias, "v_bias": v_bias, "rel_table": rel_table, "w_out": w_out, "out_bias": out_bias, "ln2_gain": ln2_gain, "ln2_bias": ln2_bias, "w_fc1": w_fc1, "fc1_bias": fc1_bias, "w_fc2": w_fc2, "fc2_bias": fc2_bias}


EPSILON = 1e-05
NEGATIVE = -1e+30

def rel_onehot():
    length = WIN * WIN
    places = jnp.arange(length)
    rowpos = places // WIN
    colpos = places % WIN
    index = (rowpos[:, None] - rowpos[None, :] + WIN - 1) * (2 * WIN - 1) + (colpos[:, None] - colpos[None, :] + WIN - 1)
    return (index.reshape(-1)[:, None] == jnp.arange(TABLE)[None, :]).astype(jnp.float32)

def window_same():
    cells = jnp.arange(SIDE)
    region = jnp.where(cells < SIDE - WIN, 0, jnp.where(cells < SIDE - SHIFT, 1, 2))
    label = region[:, None] * 3 + region[None, :]
    per_image = SIDE // WIN
    label = label.reshape(per_image, WIN, per_image, WIN).transpose(0, 2, 1, 3).reshape(-1, WIN * WIN)
    return label[:, :, None] == label[:, None, :]

def normalize(values):
    center = values - lax.optimization_barrier(jnp.mean(values, -1, keepdims=True))
    spread = lax.optimization_barrier(jnp.mean(center * center, -1, keepdims=True))
    rstd = lax.rsqrt(spread + EPSILON)
    return (center * rstd, rstd)

def norm_back(grad_hat, normal, rstd):
    return rstd * (grad_hat - lax.optimization_barrier(jnp.mean(grad_hat, -1, keepdims=True)) - normal * lax.optimization_barrier(jnp.mean(grad_hat * normal, -1, keepdims=True)))

def gelu_slope(pre):
    return 0.5 * (1.0 + lax.erf(pre * 0.7071067811865476)) + pre * jnp.exp(-0.5 * pre * pre) * 0.3989422804014327

def to_windows(tensor):
    count = tensor.shape[0]
    width = tensor.shape[-1]
    per_image = SIDE // WIN
    return tensor.reshape(count, per_image, WIN, per_image, WIN, width).transpose(0, 1, 3, 2, 4, 5).reshape(-1, width)

def from_windows(tensor, count):
    width = tensor.shape[-1]
    per_image = SIDE // WIN
    return tensor.reshape(count, per_image, per_image, WIN, WIN, width).transpose(0, 1, 3, 2, 4, 5).reshape(count, SIDE, SIDE, width)

def attention_logits(queries, keys_win, bias, same):
    scores = jnp.einsum('wqhd,wkhd->whqk', queries.astype(jnp.float32), keys_win.astype(jnp.float32))
    length = scores.shape[-1]
    scores = scores.reshape(-1, same.shape[0], HEADS, length, length) + bias[None, None]
    scores = jnp.where(same[None, :, None], scores, NEGATIVE)
    return scores.reshape(-1, HEADS, length, length)

def block_pass(pictures, cotan, used, weights, bias, onehot, same):
    gain_one, beta_one, weight_qkv, query_bias, value_bias, weight_out, proj_bias, gain_two, beta_two, weight_up, up_bias, weight_down, down_bias = weights
    f32 = jnp.float32
    bf16 = jnp.bfloat16
    count = pictures.shape[0]
    length = WIN * WIN
    head_dim = D // HEADS
    scale = head_dim ** (-0.5)
    inputs = pictures.astype(f32).reshape(-1, D)
    hat_one, rstd_one = normalize(inputs)
    normed = (hat_one * gain_one + beta_one).astype(bf16).reshape(count, SIDE, SIDE, D)
    shifted = jnp.roll(normed, (-SHIFT, -SHIFT), axis=(1, 2))
    windows = to_windows(shifted)
    qkv = jnp.dot(windows, weight_qkv, preferred_element_type=f32)
    queries = ((qkv[:, :D] + query_bias) * scale).astype(bf16).reshape(-1, length, HEADS, head_dim)
    keys_win = qkv[:, D:2 * D].astype(bf16).reshape(-1, length, HEADS, head_dim)
    values = (qkv[:, 2 * D:] + value_bias).astype(bf16).reshape(-1, length, HEADS, head_dim)
    scores = attention_logits(queries, keys_win, bias, same)
    peak = lax.optimization_barrier(jnp.max(scores, -1, keepdims=True))
    lse = peak + jnp.log(lax.optimization_barrier(jnp.sum(jnp.exp(scores - peak), -1, keepdims=True)))
    probs = jnp.exp(scores - lse).astype(bf16)
    attended = jnp.einsum('whqk,wkhd->wqhd', probs.astype(f32), values.astype(f32)).astype(bf16).reshape(-1, D)
    proj = (jnp.dot(attended, weight_out, preferred_element_type=f32) + proj_bias).astype(bf16)
    restored = jnp.roll(from_windows(proj, count), (SHIFT, SHIFT), axis=(1, 2))
    resid = inputs + restored.astype(f32).reshape(-1, D)
    hat_two, rstd_two = normalize(resid)
    normed_two = (hat_two * gain_two + beta_two).astype(bf16)
    pre = jnp.dot(normed_two, weight_up, preferred_element_type=f32) + up_bias
    act = jax.nn.gelu(pre, approximate=False).astype(bf16)
    mlp_out = jnp.dot(act, weight_down, preferred_element_type=f32) + down_bias
    used_rows = jnp.repeat(used.astype(f32), SIDE * SIDE)[:, None]
    output = (used_rows * (resid + mlp_out)).astype(bf16)
    grad_out = cotan.astype(f32).reshape(-1, D) * used_rows
    grad_low = grad_out.astype(bf16)
    grad_down = jnp.dot(act.T, grad_low, preferred_element_type=f32)
    grad_downb = lax.optimization_barrier(jnp.sum(grad_out, 0))
    grad_pre = jnp.dot(grad_low, weight_down.T, preferred_element_type=f32) * gelu_slope(pre)
    grad_upb = lax.optimization_barrier(jnp.sum(grad_pre, 0))
    grad_hidden = grad_pre.astype(bf16)
    grad_up = jnp.dot(normed_two.T, grad_hidden, preferred_element_type=f32)
    grad_normed_two = jnp.dot(grad_hidden, weight_up.T, preferred_element_type=f32)
    grad_gain_two = lax.optimization_barrier(jnp.sum(grad_normed_two * hat_two, 0))
    grad_beta_two = lax.optimization_barrier(jnp.sum(grad_normed_two, 0))
    grad_resid = grad_out + norm_back(grad_normed_two * gain_two, hat_two, rstd_two)
    grad_projb = lax.optimization_barrier(jnp.sum(grad_resid, 0))
    grad_proj = to_windows(jnp.roll(grad_resid.astype(bf16).reshape(count, SIDE, SIDE, D), (-SHIFT, -SHIFT), axis=(1, 2)))
    grad_wout = jnp.dot(attended.T, grad_proj, preferred_element_type=f32)
    grad_attended = jnp.dot(grad_proj, weight_out.T, preferred_element_type=f32).astype(bf16).reshape(-1, length, HEADS, head_dim)
    recomputed = jnp.exp(attention_logits(queries, keys_win, bias, same) - lse)
    grad_probs = jnp.einsum('wqhd,wkhd->whqk', grad_attended.astype(f32), values.astype(f32))
    grad_scores = recomputed * (grad_probs - lax.optimization_barrier(jnp.sum(recomputed * grad_probs, -1, keepdims=True)))
    grad_table = jnp.dot(lax.optimization_barrier(jnp.sum(grad_scores, 0)).reshape(HEADS, length * length), onehot, precision=lax.Precision.HIGHEST)
    grad_logits = grad_scores.astype(bf16).astype(f32)
    grad_queries = jnp.einsum('whqk,wkhd->wqhd', grad_logits, keys_win.astype(f32)).reshape(-1, D) * scale
    grad_keys = jnp.einsum('whqk,wqhd->wkhd', grad_logits, queries.astype(f32)).reshape(-1, D)
    grad_values = jnp.einsum('whqk,wqhd->wkhd', probs.astype(f32), grad_attended.astype(f32)).reshape(-1, D)
    grad_qbias = lax.optimization_barrier(jnp.sum(grad_queries, 0))
    grad_vbias = lax.optimization_barrier(jnp.sum(grad_values, 0))
    grad_qkv = jnp.concatenate([grad_queries, grad_keys, grad_values], axis=1).astype(bf16)
    grad_wqkv = jnp.dot(windows.T, grad_qkv, preferred_element_type=f32)
    grad_shifted = jnp.dot(grad_qkv, weight_qkv.T, preferred_element_type=f32).astype(bf16)
    grad_normed = jnp.roll(from_windows(grad_shifted, count), (SHIFT, SHIFT), axis=(1, 2)).astype(f32).reshape(-1, D)
    grad_gain_one = lax.optimization_barrier(jnp.sum(grad_normed * hat_one, 0))
    grad_beta_one = lax.optimization_barrier(jnp.sum(grad_normed, 0))
    grad_input = grad_resid + norm_back(grad_normed * gain_one, hat_one, rstd_one)
    grads = (grad_gain_one, grad_beta_one, grad_wqkv, grad_qbias, grad_vbias, grad_table, grad_wout, grad_projb, grad_gain_two, grad_beta_two, grad_up, grad_upb, grad_down, grad_downb)
    return (output.reshape(count, SIDE, SIDE, D), grad_input.reshape(count, SIDE, SIDE, D), grads)

def reference(block_input, slot_used, cotangent, ln1_gain, ln1_bias, w_qkv, q_bias, v_bias, rel_table, w_out, out_bias, ln2_gain, ln2_bias, w_fc1, fc1_bias, w_fc2, fc2_bias):
    f32 = jnp.float32
    weights = (ln1_gain.astype(f32), ln1_bias.astype(f32), w_qkv, q_bias.astype(f32), v_bias.astype(f32), w_out, out_bias.astype(f32), ln2_gain.astype(f32), ln2_bias.astype(f32), w_fc1, fc1_bias.astype(f32), w_fc2, fc2_bias.astype(f32))
    onehot = rel_onehot()
    same = window_same()
    length = WIN * WIN
    bias = jnp.dot(rel_table.astype(f32), onehot.T, precision=lax.Precision.HIGHEST).reshape(HEADS, length, length)
    images = block_input.reshape(GROUPS, SLOTS, SIDE, SIDE, D)
    cotans = cotangent.reshape(GROUPS, SLOTS, SIDE, SIDE, D)
    shapes = (ln1_gain, ln1_bias, w_qkv, q_bias, v_bias, rel_table, w_out, out_bias, ln2_gain, ln2_bias, w_fc1, fc1_bias, w_fc2, fc2_bias)
    zeros = tuple((jnp.zeros(param.shape, f32) for param in shapes))

    def visit(totals, inputs):
        pictures, cotan, used = inputs
        output, grad_input, grads = block_pass(pictures, cotan, used, weights, bias, onehot, same)
        return (tuple((left + right for left, right in zip(totals, grads))), (output, grad_input))
    totals, (outputs, grad_inputs) = lax.scan(visit, zeros, (images, cotans, slot_used))
    t01, t02, t03, t04, t05, t06, t07, t08, t09, t10, t11, t12, t13, t14 = totals
    return (outputs.reshape(IMAGES, SIDE, SIDE, D), grad_inputs.reshape(IMAGES, SIDE, SIDE, D), t01, t02, t03, t04, t05, t06, t07, t08, t09, t10, t11, t12, t13, t14)
```

```python
import functools

import jax
import jax.numpy as jnp
from jax import lax
from jax.experimental import pallas as pl
from jax.experimental.pallas import tpu as pltpu
from jax.sharding import PartitionSpec as P

D = 512
HEADS = 16
WIN = 7
SHIFT = 3
SIDE = 14
TABLE = 169
LEN = WIN * WIN
EPSILON = 1e-05
NEGATIVE = -1e30

PAD = 56
SEG = 64
PIC = 2 * PAD
COLS = 16
QUAD = 4
GROUPS = HEADS // QUAD
LANES = 128
HEAD = D // HEADS
SCALE = HEAD ** (-0.5)
OWN = WIN - SHIFT

f32 = jnp.float32
bf16 = jnp.bfloat16


def partner(value, axis, bit):
    mask = 1 << bit
    pairs = [(source, source ^ mask) for source in range(lax.axis_size(axis))]
    return lax.ppermute(value, axis, pairs)


def bits_of(axis):
    return (lax.axis_size(axis) - 1).bit_length()


def nt(left, right):
    return lax.dot_general(left, right, (((1,), (1,)), ((), ())), preferred_element_type=f32)


def nn(left, right):
    return jnp.dot(left, right, preferred_element_type=f32)


def tn(left, right):
    return lax.dot_general(left, right, (((0,), (0,)), ((), ())), preferred_element_type=f32)


def stats(values):
    center = values - jnp.mean(values, -1, keepdims=True)
    rstd = lax.rsqrt(jnp.mean(center * center, -1, keepdims=True) + EPSILON)
    return center * rstd, rstd


def norm_back(grad_hat, normal, rstd):
    return rstd * (
        grad_hat
        - jnp.mean(grad_hat, -1, keepdims=True)
        - normal * jnp.mean(grad_hat * normal, -1, keepdims=True)
    )


def rowsum(values):
    return jnp.sum(values, 0, keepdims=True)


def load_shards(owners, refs, target, sems):
    rows = refs[0].shape[0]
    copies = []
    for at, ref in enumerate(refs):
        start = pl.multiple_of(owners[at] * rows, rows)
        copies.append(pltpu.make_async_copy(ref, target.at[pl.ds(start, rows)], sems.at[at]))
    return copies


def stage_rows(stage, own_ref, recv_ref, image):
    for row in range(OWN):
        stage[image, row, :SIDE, :] = own_ref[image, SHIFT + row]
    for row in range(SHIFT):
        stage[image, OWN + row, :SIDE, :] = recv_ref[image, row]


def to_windows(stage, perm, image):
    flat = stage[image].reshape(WIN * COLS, D)
    return nn(perm, flat)


def pad_rows(values):
    return jnp.concatenate([values, jnp.zeros((SEG - PAD, values.shape[1]), f32)], axis=0)


def head_masks(dtype):
    lane = lax.broadcasted_iota(jnp.int32, (SEG, LANES), 1) // HEAD
    return [jnp.where(lane == head, 1.0, 0.0).astype(dtype) for head in range(QUAD)]


def spread(block, masks):
    return jnp.concatenate([block * mask for mask in masks], axis=0)


def forward_attention(
    owners, own_ref, recv_ref, perm_ref, vec_ref, table_ref, *rest, shards, pics
):
    weight_refs = rest[:shards]
    xw_ref, qkv_ref, att_ref, weight, stage, proj, sems = rest[shards:]

    @pl.when(pl.program_id(0) == 0)
    def _():
        copies = load_shards(owners, weight_refs, weight, sems)
        for copy in copies:
            copy.start()
        stage[...] = jnp.zeros_like(stage)
        for copy in copies:
            copy.wait()

    perm = perm_ref[...]
    gain = vec_ref[0:1]
    beta = vec_ref[1:2]
    qb = vec_ref[2:3]
    vb = vec_ref[3:4]
    for image in range(pics):
        stage_rows(stage, own_ref, recv_ref, image)
        values = to_windows(stage, perm, image)
        rows = pl.ds(image * PIC, PIC)
        xw_ref[rows] = values.astype(bf16)
        hat, _ = stats(values)
        normed = (hat * gain + beta).astype(bf16)
        proj[rows, 0:D] = ((nn(normed, weight[:, 0:D]) + qb) * SCALE)
        proj[rows, D : 2 * D] = nn(normed, weight[:, D : 2 * D])
        proj[rows, 2 * D :] = nn(normed, weight[:, 2 * D :]) + vb
    qkv_ref[...] = proj[...].astype(bf16)

    masks = head_masks(bf16)
    half = lax.broadcasted_iota(jnp.int32, (PAD, LANES), 1) < SEG
    row_head = lax.broadcasted_iota(jnp.int32, (QUAD * SEG, LANES), 0) // SEG
    lane_head = lax.broadcasted_iota(jnp.int32, (QUAD * SEG, LANES), 1) // HEAD
    ones = jnp.where(row_head == lane_head, 1.0, 0.0).astype(bf16)

    def image_step(image, carry):
        for window in range(2):
            start = pl.multiple_of(image * PIC + window * PAD, 8)
            rows = pl.ds(start, PAD)
            for group in range(GROUPS):
                at = group * LANES
                query = pad_rows(proj[rows, at : at + LANES]).astype(bf16)
                key = pad_rows(proj[rows, D + at : D + at + LANES]).astype(bf16)
                value = pad_rows(proj[rows, 2 * D + at : 2 * D + at + LANES]).astype(bf16)
                scores = nt(query, spread(key, masks))[:PAD] + table_ref[window, group]
                parts = []
                for side in range(2):
                    block = scores[:, side * LANES : (side + 1) * LANES]
                    low = jnp.max(jnp.where(half, block, NEGATIVE), -1, keepdims=True)
                    high = jnp.max(jnp.where(half, NEGATIVE, block), -1, keepdims=True)
                    parts.append(jnp.exp(block - jnp.where(half, low, high)))
                probs = pad_rows(jnp.concatenate(parts, axis=1)).astype(bf16)
                right = jnp.concatenate([spread(value, masks), ones], axis=1)
                both = nn(probs, right)[:PAD]
                mixed = both[:, :LANES] / both[:, LANES:]
                att_ref[rows, at : at + LANES] = mixed.astype(bf16)
        return carry

    lax.fori_loop(0, pics, image_step, 0)


def middle(
    owners, used, own_ref, recv_ref, xw_ref, att_ref, perm_ref, back_ref, vec_ref, upb_ref,
    *rest, shards, pics
):
    out_refs = rest[: 3 * shards]
    wo_refs, w1_refs, w2_refs = out_refs[:shards], out_refs[shards : 2 * shards], out_refs[2 * shards :]
    (
        keep_ref, send_ref, resid_ref, datt_ref, gw1_ref, gw2_ref, gwo_ref, vecg_ref, upg_ref,
        wo, w1, w2, stage, n2s, cts, gn2s, mlps, acc1, acc2, acco, sems,
    ) = rest[3 * shards :]
    step = pl.program_id(0)
    last = pl.num_programs(0) - 1

    @pl.when(step == 0)
    def _():
        copies = (
            load_shards(owners, wo_refs, wo, sems.at[0])
            + load_shards(owners, w1_refs, w1, sems.at[1])
            + load_shards(owners, w2_refs, w2, sems.at[2])
        )
        for copy in copies:
            copy.start()
        stage[...] = jnp.zeros_like(stage)
        acc1[...] = jnp.zeros_like(acc1)
        acc2[...] = jnp.zeros_like(acc2)
        acco[...] = jnp.zeros_like(acco)
        vecg_ref[...] = jnp.zeros_like(vecg_ref)
        upg_ref[...] = jnp.zeros_like(upg_ref)
        for copy in copies:
            copy.wait()

    perm = perm_ref[...]
    back = back_ref[...]
    pbias = vec_ref[4:5]
    gain = vec_ref[5:6]
    beta = vec_ref[6:7]
    dbias = vec_ref[7:8]
    rows_all = pics * PIC
    for image in range(pics):
        stage_rows(stage, own_ref, recv_ref, image)
        flag = used[step * pics + image].astype(f32)
        rows = pl.ds(image * PIC, PIC)
        cts[rows] = (to_windows(stage, perm, image) * flag).astype(bf16)
    proj = (nn(att_ref[...], wo[...]) + pbias).astype(bf16)
    resid = xw_ref[...].astype(f32) + proj.astype(f32)
    hat, rstd = stats(resid)
    n2s[...] = (hat * gain + beta).astype(bf16)
    mlps[...] = resid + dbias
    gn2s[...] = jnp.zeros_like(gn2s)
    n2t = n2s[...].T
    ctt = cts[...].T
    span = w1.shape[1] // 4

    def chunk(index, carry):
        cols = pl.ds(pl.multiple_of(index * span, span), span)
        pre = nn(n2s[...], w1[:, cols]) + upb_ref[0:1, cols]
        dact = nt(cts[...], w2[cols, :])
        phi = 0.5 * (1.0 + lax.erf(pre * 0.7071067811865476))
        act = (pre * phi).astype(bf16)
        slope = phi + pre * jnp.exp(-0.5 * pre * pre) * 0.3989422804014327
        gpre = dact * slope
        upg_ref[0:1, cols] += rowsum(gpre)
        hidden = gpre.astype(bf16)
        mlps[...] += nn(act, w2[cols, :])
        gn2s[...] += nt(hidden, w1[:, cols])
        acc2[:, cols] += nn(ctt, act)
        acc1[:, cols] += nn(n2t, hidden)
        return carry

    lax.fori_loop(0, 4, chunk, 0)

    gn2 = gn2s[...]
    ct = cts[...].astype(f32)
    gresid = ct + norm_back(gn2 * gain, hat, rstd)
    vecg_ref[4:5] += rowsum(gresid)
    vecg_ref[5:6] += rowsum(gn2 * hat)
    vecg_ref[6:7] += rowsum(gn2)
    vecg_ref[7:8] += rowsum(ct)
    low = gresid.astype(bf16)
    resid_ref[...] = low
    datt_ref[...] = nt(low, wo[...]).astype(bf16)
    acco[...] += tn(att_ref[...], low)
    for image in range(pics):
        flag = used[step * pics + image].astype(f32)
        rows = pl.ds(image * PIC, PIC)
        mine = (mlps[rows] * flag).astype(bf16)
        framed = nn(back, mine).astype(bf16).reshape(WIN, COLS, D)
        for row in range(OWN):
            keep_ref[image, SHIFT + row] = framed[row, :SIDE]
        for row in range(SHIFT):
            keep_ref[image, row] = framed[OWN + row, :SIDE]
            send_ref[image, row] = framed[OWN + row, :SIDE]

    @pl.when(step == last)
    def _():
        gwo_ref[...] = acco[...].astype(bf16)
        gw1_ref[...] = acc1[...].astype(bf16)
        for piece in range(4):
            cols = slice(piece * span, (piece + 1) * span)
            gw2_ref[cols, :] = acc2[:, cols].T.astype(bf16)


def backward_attention(
    owners, xw_ref, qkv_ref, resid_ref, datt_ref, back_ref, vec_ref, table_ref,
    *rest, shards, pics
):
    weight_refs = rest[:shards]
    (
        keep_ref, send_ref, gw_ref, vecg_ref, tab_ref, weight, dqkv, acc, sems,
    ) = rest[shards:]
    step = pl.program_id(0)
    last = pl.num_programs(0) - 1

    @pl.when(step == 0)
    def _():
        copies = load_shards(owners, weight_refs, weight, sems)
        for copy in copies:
            copy.start()
        acc[...] = jnp.zeros_like(acc)
        vecg_ref[...] = jnp.zeros_like(vecg_ref)
        tab_ref[...] = jnp.zeros_like(tab_ref)
        for copy in copies:
            copy.wait()

    masks = head_masks(bf16)
    picks = head_masks(f32)

    def image_step(image, carry):
        for window in range(2):
            start = pl.multiple_of(image * PIC + window * PAD, 8)
            rows = pl.ds(start, PAD)
            for group in range(GROUPS):
                at = group * LANES
                query = pad_rows(qkv_ref[rows, at : at + LANES].astype(f32)).astype(bf16)
                key = pad_rows(qkv_ref[rows, D + at : D + at + LANES].astype(f32)).astype(bf16)
                value = pad_rows(
                    qkv_ref[rows, 2 * D + at : 2 * D + at + LANES].astype(f32)
                ).astype(bf16)
                datt = pad_rows(datt_ref[rows, at : at + LANES].astype(f32)).astype(bf16)
                queries = spread(query, masks)
                datts = spread(datt, masks)
                scores = nt(key, queries)[:PAD] + table_ref[window, group]
                shifted = jnp.exp(scores - jnp.max(scores, 0, keepdims=True))
                probs = shifted * (1.0 / jnp.sum(shifted, 0, keepdims=True))
                dprobs = nt(value, datts)[:PAD]
                inner = jnp.sum(probs * dprobs, 0, keepdims=True)
                dscores = probs * (dprobs - inner)
                tab_ref[group] += dscores
                dlow = pad_rows(dscores).astype(bf16)
                plow = pad_rows(probs).astype(bf16)
                dkey = nn(dlow, queries)[:PAD]
                dvalue = nn(plow, datts)[:PAD]
                tall = tn(dlow, key)
                dquery = tall[0:PAD] * picks[0][:PAD]
                for head in range(1, QUAD):
                    dquery += tall[head * SEG : head * SEG + PAD] * picks[head][:PAD]
                dqkv[rows, at : at + LANES] = dquery * SCALE
                dqkv[rows, D + at : D + at + LANES] = dkey
                dqkv[rows, 2 * D + at : 2 * D + at + LANES] = dvalue
        return carry

    lax.fori_loop(0, pics, image_step, 0)

    gain = vec_ref[0:1]
    beta = vec_ref[1:2]
    hat, rstd = stats(xw_ref[...].astype(f32))
    normed = (hat * gain + beta).astype(bf16)
    vecg_ref[2:3] += rowsum(dqkv[:, 0:D])
    vecg_ref[3:4] += rowsum(dqkv[:, 2 * D :])
    low = dqkv[...].astype(bf16)
    acc[...] += tn(normed, low)
    gnormed = nt(low, weight[...]).astype(bf16).astype(f32)
    vecg_ref[0:1] += rowsum(gnormed * hat)
    vecg_ref[1:2] += rowsum(gnormed)
    ginput = resid_ref[...].astype(f32) + norm_back(gnormed * gain, hat, rstd)
    glow = ginput.astype(bf16)
    back = back_ref[...]
    for image in range(pics):
        framed = nn(back, glow[image * PIC : (image + 1) * PIC]).reshape(WIN, COLS, D)
        for row in range(OWN):
            keep_ref[image, SHIFT + row] = framed[row, :SIDE]
        for row in range(SHIFT):
            keep_ref[image, row] = framed[OWN + row, :SIDE]
            send_ref[image, row] = framed[OWN + row, :SIDE].astype(bf16)

    @pl.when(step == last)
    def _():
        gw_ref[...] = acc[...].astype(bf16)


def gather(piece):
    held = [piece]
    for bit in reversed(range(bits_of("fsdp"))):
        held = held + [partner(one, "fsdp", bit) for one in held]
    return held


def held_masks():
    masks = [0]
    for bit in reversed(range(bits_of("fsdp"))):
        masks = masks + [mask | (1 << bit) for mask in masks]
    return masks


def in_order(held, me):
    masks = held_masks()
    count = len(held)
    table = [None] * count
    for mask, piece in zip(masks, held):
        table[mask] = piece
    stacked = jnp.stack(table)
    for bit in range(bits_of("fsdp")):
        split = stacked.reshape(count >> (bit + 1), 2, 1 << bit, *stacked.shape[1:])
        swap = (me >> bit) & 1
        split = jnp.where(swap == 1, split[:, ::-1], split)
        stacked = split.reshape(stacked.shape)
    return stacked


def reduce_owned(grad, me):
    ranks = lax.axis_size("fsdp")
    own = grad.reshape(ranks, grad.shape[0] // ranks, grad.shape[1])
    for bit in range(bits_of("fsdp")):
        pairs = own.reshape(own.shape[0] // 2, 2, *own.shape[1:])
        mine = (me >> bit) & 1
        keep = lax.dynamic_index_in_dim(pairs, mine, 1, keepdims=False)
        send = lax.dynamic_index_in_dim(pairs, 1 - mine, 1, keepdims=False)
        got = partner(send, "fsdp", bit)
        own = (keep.astype(f32) + got.astype(f32)).astype(bf16)
    own = own[0]
    for axis in ("band", "img"):
        for bit in range(bits_of(axis)):
            own = (own.astype(f32) + partner(own, axis, bit).astype(f32)).astype(bf16)
    return own.astype(f32)


def reduce_small(flat):
    for axis in ("fsdp", "band", "img"):
        for bit in range(bits_of(axis)):
            flat = flat + partner(flat, axis, bit)
    return flat


def window_tables(table):
    places = jnp.arange(PAD)
    other = jnp.arange(SEG)
    rowq, colq = places // WIN, places % WIN
    rowk, colk = other // WIN, other % WIN
    index = (rowq[:, None] - rowk[None, :] + WIN - 1) * (2 * WIN - 1) + (
        colq[:, None] - colk[None, :] + WIN - 1
    )
    real = (places[:, None] < LEN) & (other[None, :] < LEN)
    index = jnp.where(real, index, TABLE)
    flip = (rowk[None, :] - rowq[:, None] + WIN - 1) * (2 * WIN - 1) + (
        colk[None, :] - colq[:, None] + WIN - 1
    )
    flip = jnp.where(real, flip, TABLE)
    one = (index[..., None] == jnp.arange(TABLE)).astype(bf16)
    two = (flip[..., None] == jnp.arange(TABLE)).astype(bf16)
    return one, two


def regions(band):
    cells = jnp.arange(SIDE)
    region = jnp.where(cells < SIDE - WIN, 0, jnp.where(cells < SIDE - SHIFT, 1, 2))
    rows = lax.dynamic_slice_in_dim(region, band * WIN, WIN)
    cols = region.reshape(SIDE // WIN, WIN)
    label = rows[None, :, None] * 3 + cols[:, None, :]
    return label.reshape(SIDE // WIN, LEN)


def shards(
    block_input,
    slot_used,
    cotangent,
    ln1_gain,
    ln1_bias,
    w_qkv,
    q_bias,
    v_bias,
    rel_table,
    w_out,
    out_bias,
    ln2_gain,
    ln2_bias,
    w_fc1,
    fc1_bias,
    w_fc2,
    fc2_bias,
):
    slots = block_input.shape[0]
    pics = 4
    steps = slots // pics
    rows = pics * PIC
    ranks = lax.axis_size("fsdp")
    width = w_fc1.shape[1]
    me = lax.axis_index("fsdp")
    band = lax.axis_index("band")
    owners = jnp.stack([me ^ mask for mask in held_masks()]).astype(jnp.int32)

    held_qkv = gather(w_qkv)
    pieces = (
        ln1_gain, ln1_bias, q_bias, v_bias, out_bias, ln2_gain, ln2_bias, fc2_bias,
        fc1_bias, rel_table.reshape(-1),
    )
    small = in_order(gather(jnp.concatenate(pieces)), me)
    arrived = partner(block_input[:, :SHIFT], "band", 0)
    per = ln1_gain.shape[0]
    vectors = small[:, : 8 * per].reshape(ranks, 8, per).transpose(1, 0, 2).reshape(8, D).astype(f32)
    ups = fc1_bias.shape[0]
    up_bias = small[:, 8 * per : 8 * per + ups].reshape(1, width).astype(f32)
    table = small[:, 8 * per + ups :].reshape(HEADS, TABLE)

    later = lax.optimization_barrier((w_out, w_fc1, w_fc2, cotangent[:, :SHIFT], held_qkv[-1], arrived))
    held_out = gather(later[0])
    held_up = gather(later[1])
    held_down = gather(later[2])
    ct_arrived = partner(later[3], "band", 0)

    one, two = window_tables(table)
    label = regions(band)
    label_q = jnp.pad(label, ((0, 0), (0, PAD - LEN)), constant_values=-1)
    label_k = jnp.pad(label, ((0, 0), (0, SEG - LEN)), constant_values=-1)
    differ = label_q[:, :, None] != label_k[:, None, :]
    spot = jnp.arange(SEG)
    block_f = jnp.where(differ | (spot[None, None, :] >= LEN), NEGATIVE, 0.0).astype(f32)
    block_b = jnp.where(
        (differ & (spot[None, None, :] < LEN)) | (jnp.arange(PAD)[None, :, None] >= LEN), NEGATIVE, 0.0
    ).astype(f32)
    quads = table.reshape(GROUPS, QUAD, TABLE)
    bias_f = jnp.einsum("ght,ijt->gihj", quads, one, preferred_element_type=f32)
    bias_b = jnp.einsum("ght,ijt->gihj", quads, two, preferred_element_type=f32)
    table_f = (bias_f[None] + block_f[:, None, :, None, :]).reshape(2, GROUPS, PAD, QUAD * SEG)
    table_b = (bias_b[None] + block_b[:, None, :, None, :]).reshape(2, GROUPS, PAD, QUAD * SEG)

    target = jnp.arange(PIC)
    window, spot_in = target // PAD, target % PAD
    source = (spot_in // WIN) * COLS + (window * WIN + spot_in % WIN + SHIFT) % SIDE
    source = jnp.where(spot_in < LEN, source, -1)
    perm = (source[:, None] == jnp.arange(WIN * COLS)[None, :]).astype(bf16)
    back = (source[None, :] == jnp.arange(WIN * COLS)[:, None]).astype(bf16)

    any_spec = pl.BlockSpec(memory_space=pl.ANY)

    def whole(shape):
        return pl.BlockSpec(shape, lambda i, *_: (0,) * len(shape))

    pic_spec = pl.BlockSpec((pics, WIN, SIDE, D), lambda i, *_: (i, 0, 0, 0))
    arr_spec = pl.BlockSpec((pics, SHIFT, SIDE, D), lambda i, *_: (i, 0, 0, 0))

    def row_spec(cols):
        return pl.BlockSpec((rows, cols), lambda i, *_: (i, 0))

    total = slots * PIC
    params = pltpu.CompilerParams(
        dimension_semantics=("arbitrary",), vmem_limit_bytes=60 * 1024 * 1024
    )

    xw, qkv, att = pl.pallas_call(
        functools.partial(forward_attention, shards=ranks, pics=pics),
        grid_spec=pltpu.PrefetchScalarGridSpec(
            num_scalar_prefetch=1,
            grid=(steps,),
            in_specs=[
                pic_spec, arr_spec, whole((PIC, PIC)), whole((8, D)),
                whole((2, GROUPS, PAD, QUAD * SEG)),
            ] + [any_spec] * ranks,
            out_specs=[row_spec(D), row_spec(3 * D), row_spec(D)],
            scratch_shapes=[
                pltpu.VMEM((D, 3 * D), bf16),
                pltpu.VMEM((pics, WIN, COLS, D), bf16),
                pltpu.VMEM((rows, 3 * D), f32),
                pltpu.SemaphoreType.DMA((ranks,)),
            ],
        ),
        out_shape=[
            jax.ShapeDtypeStruct((total, D), bf16),
            jax.ShapeDtypeStruct((total, 3 * D), bf16),
            jax.ShapeDtypeStruct((total, D), bf16),
        ],
        compiler_params=params,
        name="attention_forward",
    )(owners, block_input, arrived, perm, vectors, table_f, *held_qkv)

    keep, send, resid, datt, gw1, gw2, gwo, vecg, upg = pl.pallas_call(
        functools.partial(middle, shards=ranks, pics=pics),
        grid_spec=pltpu.PrefetchScalarGridSpec(
            num_scalar_prefetch=2,
            grid=(steps,),
            in_specs=[
                pic_spec, arr_spec, row_spec(D), row_spec(D), whole((PIC, PIC)),
                whole((PIC, PIC)), whole((8, D)), whole((1, width)),
            ] + [any_spec] * (3 * ranks),
            out_specs=[
                pic_spec, arr_spec, row_spec(D), row_spec(D), whole((D, width)),
                whole((width, D)), whole((D, D)), whole((8, D)), whole((1, width)),
            ],
            scratch_shapes=[
                pltpu.VMEM((D, D), bf16),
                pltpu.VMEM((D, width), bf16),
                pltpu.VMEM((width, D), bf16),
                pltpu.VMEM((pics, WIN, COLS, D), bf16),
                pltpu.VMEM((rows, D), bf16),
                pltpu.VMEM((rows, D), bf16),
                pltpu.VMEM((rows, D), f32),
                pltpu.VMEM((rows, D), f32),
                pltpu.VMEM((D, width), f32),
                pltpu.VMEM((D, width), f32),
                pltpu.VMEM((D, D), f32),
                pltpu.SemaphoreType.DMA((3, ranks)),
            ],
        ),
        out_shape=[
            jax.ShapeDtypeStruct((slots, WIN, SIDE, D), bf16),
            jax.ShapeDtypeStruct((slots, SHIFT, SIDE, D), bf16),
            jax.ShapeDtypeStruct((total, D), bf16),
            jax.ShapeDtypeStruct((total, D), bf16),
            jax.ShapeDtypeStruct((D, width), bf16),
            jax.ShapeDtypeStruct((width, D), bf16),
            jax.ShapeDtypeStruct((D, D), bf16),
            jax.ShapeDtypeStruct((8, D), f32),
            jax.ShapeDtypeStruct((1, width), f32),
        ],
        compiler_params=params,
        name="mlp_both",
    )(
        owners, slot_used.reshape(-1), cotangent, ct_arrived, xw, att, perm, back, vectors, up_bias,
        *held_out, *held_up, *held_down,
    )
    output = lax.dynamic_update_slice(keep, partner(send, "band", 0), (0, 0, 0, 0))

    gkeep, gsend, gwq, vecg1, tab = pl.pallas_call(
        functools.partial(backward_attention, shards=ranks, pics=pics),
        grid_spec=pltpu.PrefetchScalarGridSpec(
            num_scalar_prefetch=1,
            grid=(steps,),
            in_specs=[
                row_spec(D), row_spec(3 * D), row_spec(D), row_spec(D), whole((PIC, PIC)),
                whole((8, D)), whole((2, GROUPS, PAD, QUAD * SEG)),
            ] + [any_spec] * ranks,
            out_specs=[
                pic_spec, arr_spec, whole((D, 3 * D)), whole((8, D)),
                whole((GROUPS, PAD, QUAD * SEG)),
            ],
            scratch_shapes=[
                pltpu.VMEM((D, 3 * D), bf16),
                pltpu.VMEM((rows, 3 * D), f32),
                pltpu.VMEM((D, 3 * D), f32),
                pltpu.SemaphoreType.DMA((ranks,)),
            ],
        ),
        out_shape=[
            jax.ShapeDtypeStruct((slots, WIN, SIDE, D), f32),
            jax.ShapeDtypeStruct((slots, SHIFT, SIDE, D), bf16),
            jax.ShapeDtypeStruct((D, 3 * D), bf16),
            jax.ShapeDtypeStruct((8, D), f32),
            jax.ShapeDtypeStruct((GROUPS, PAD, QUAD * SEG), f32),
        ],
        compiler_params=params,
        name="attention_backward",
    )(owners, xw, qkv, resid, datt, back, vectors, table_b, *held_qkv)
    grad_input = lax.dynamic_update_slice(
        gkeep, partner(gsend, "band", 0).astype(f32), (0, 0, 0, 0)
    )

    own_up = reduce_owned(gw1, me)
    own_down = reduce_owned(gw2, me)
    own_out = reduce_owned(gwo, me)
    own_qkv = reduce_owned(gwq, me)
    spots = tab.reshape(GROUPS, PAD, QUAD, SEG)
    grad_table = jnp.einsum(
        "gihj,ijt->ght", spots, two.astype(f32), precision=lax.Precision.HIGHEST
    )
    flat = reduce_small(
        jnp.concatenate([vecg1[:4].reshape(-1), vecg[4:].reshape(-1), upg.reshape(-1), grad_table.reshape(-1)])
    )
    lanes = flat[: 8 * D].reshape(8, ranks, per)
    mine = lax.dynamic_index_in_dim(lanes, me, 1, keepdims=False)
    own_upb = lax.dynamic_slice_in_dim(flat, 8 * D + me * ups, ups)
    heads = rel_table.shape[0]
    own_table = lax.dynamic_slice_in_dim(flat, 8 * D + width + me * heads * TABLE, heads * TABLE)
    return (
        output,
        grad_input,
        mine[0],
        mine[1],
        own_qkv,
        mine[2],
        mine[3],
        own_table.reshape(heads, TABLE),
        own_out,
        mine[4],
        mine[5],
        mine[6],
        own_up,
        own_upb,
        own_down,
        mine[7],
    )


def solution(mesh):
    pictures = P(("img", "fsdp"), "band", None, None)
    flat = P("fsdp")
    wide = P("fsdp", None)
    return jax.shard_map(
        shards,
        mesh=mesh,
        in_specs=(
            pictures, P(("img", "fsdp"), None), pictures, flat, flat, wide, flat, flat, wide, wide,
            flat, flat, flat, wide, flat, wide, flat,
        ),
        out_specs=(
            pictures, pictures, flat, flat, wide, flat, flat, wide, wide, flat, flat, flat, wide,
            flat, wide, flat,
        ),
        check_vma=False,
    )
```

```python
import functools

import jax
import jax.numpy as jnp
import numpy as np
from jax import lax
from jax.experimental import pallas as pl
from jax.experimental.pallas import tpu as pltpu
from jax.sharding import PartitionSpec as P


D = 512
HEADS = 16
WIN = 7
SHIFT = 3
SIDE = 14
TABLE = 169
LEN = WIN * WIN
EPSILON = 1e-05
NEGATIVE = -1e30

PAD = 56
SEG = 64
PIC = 2 * PAD
COLS = 16
QUAD = 4
GROUPS = HEADS // QUAD
LANES = 128
HEAD = D // HEADS
SCALE = HEAD ** (-0.5)
OWN = WIN - SHIFT

MICRO_FLOPS = 1.15e9
MICRO_BYTES = 3.0e6

f32 = jnp.float32
bf16 = jnp.bfloat16


def partner(value, axis, bit):
    mask = 1 << bit
    pairs = [(source, source ^ mask) for source in range(lax.axis_size(axis))]
    return lax.ppermute(value, axis, pairs)


def bits_of(axis):
    return (lax.axis_size(axis) - 1).bit_length()


def nt(left, right):
    return lax.dot_general(left, right, (((1,), (1,)), ((), ())), preferred_element_type=f32)


def nn(left, right):
    return jnp.dot(left, right, preferred_element_type=f32)


def tn(left, right):
    return lax.dot_general(left, right, (((0,), (0,)), ((), ())), preferred_element_type=f32)


def stats(values):
    center = values - jnp.mean(values, -1, keepdims=True)
    rstd = lax.rsqrt(jnp.mean(center * center, -1, keepdims=True) + EPSILON)
    return center * rstd, rstd


def norm_back(grad_hat, normal, rstd):
    return rstd * (
        grad_hat
        - jnp.mean(grad_hat, -1, keepdims=True)
        - normal * jnp.mean(grad_hat * normal, -1, keepdims=True)
    )


def rowsum(values):
    return jnp.sum(values, 0, keepdims=True)


def load_shards(owners, refs, target, sems):
    rows = refs[0].shape[0]
    copies = []
    for at, ref in enumerate(refs):
        start = pl.multiple_of(owners[at] * rows, rows)
        copies.append(pltpu.make_async_copy(ref, target.at[pl.ds(start, rows)], sems.at[at]))
    return copies


def stage_rows(stage, own_ref, recv_ref, image):
    for row in range(OWN):
        stage[image, row, :SIDE, :] = own_ref[image, SHIFT + row]
    for row in range(SHIFT):
        stage[image, OWN + row, :SIDE, :] = recv_ref[image, row]


def to_windows(stage, perm, image):
    flat = stage[image].reshape(WIN * COLS, D)
    return nn(perm, flat)


def pad_rows(values):
    return jnp.concatenate([values, jnp.zeros((SEG - PAD, values.shape[1]), f32)], axis=0)


def head_masks(dtype):
    lane = lax.broadcasted_iota(jnp.int32, (SEG, LANES), 1) // HEAD
    return [jnp.where(lane == head, 1.0, 0.0).astype(dtype) for head in range(QUAD)]


def spread(block, masks):
    return jnp.concatenate([block * mask for mask in masks], axis=0)


def forward_attention(
    owners, own_ref, recv_ref, perm_ref, vec_ref, table_ref, *rest, shards, pics, chained
):
    weight_refs = rest[:shards]
    rest = rest[shards + (3 if chained else 0) :]
    xw_ref, qkv_ref, att_ref, weight, stage, norms, sems = rest

    @pl.when(pl.program_id(0) == 0)
    def _():
        copies = load_shards(owners, weight_refs, weight, sems)
        for copy in copies:
            copy.start()
        stage[...] = jnp.zeros_like(stage)
        for copy in copies:
            copy.wait()

    perm = perm_ref[...]
    gain = vec_ref[0:1]
    beta = vec_ref[1:2]
    for image in range(pics):
        stage_rows(stage, own_ref, recv_ref, image)
        values = to_windows(stage, perm, image)
        rows = pl.ds(image * PIC, PIC)
        xw_ref[rows] = values.astype(bf16)
        hat, _ = stats(values)
        norms[rows] = (hat * gain + beta).astype(bf16)
    normed = norms[...]
    for part in range(3):
        product = nn(normed, weight[:, part * D : (part + 1) * D])
        if part == 0:
            product = (product + vec_ref[2:3]) * SCALE
        if part == 2:
            product = product + vec_ref[3:4]
        for window in range(2 * pics):
            qkv_ref[window, :PAD, part * D : (part + 1) * D] = product[
                window * PAD : (window + 1) * PAD
            ].astype(bf16)
    for window in range(2 * pics):
        qkv_ref[window, PAD:] = jnp.zeros((SEG - PAD, 3 * D), bf16)

    masks = head_masks(bf16)
    half = lax.broadcasted_iota(jnp.int32, (PAD, LANES), 1) < SEG
    row_head = lax.broadcasted_iota(jnp.int32, (QUAD * SEG, LANES), 0) // SEG
    lane_head = lax.broadcasted_iota(jnp.int32, (QUAD * SEG, LANES), 1) // HEAD
    ones = jnp.where(row_head == lane_head, 1.0, 0.0).astype(bf16)
    units = 2 * GROUPS

    def image_step(image, carry):
        state = [None] * units

        def begin(unit):
            window, group = divmod(unit, GROUPS)
            at = group * LANES
            place = image * 2 + window
            query = qkv_ref[place, :, at : at + LANES]
            key = qkv_ref[place, :, D + at : D + at + LANES]
            state[unit] = nt(query, spread(key, masks))[:PAD]

        def soften(unit):
            window, group = divmod(unit, GROUPS)
            scores = state[unit] + table_ref[window, group]
            parts = []
            for side in range(2):
                block = scores[:, side * LANES : (side + 1) * LANES]
                low = jnp.max(jnp.where(half, block, NEGATIVE), -1, keepdims=True)
                high = jnp.max(jnp.where(half, NEGATIVE, block), -1, keepdims=True)
                parts.append(jnp.exp(block - jnp.where(half, low, high)))
            state[unit] = pad_rows(jnp.concatenate(parts, axis=1)).astype(bf16)

        def mix(unit):
            window, group = divmod(unit, GROUPS)
            at = group * LANES
            value = qkv_ref[image * 2 + window, :, 2 * D + at : 2 * D + at + LANES]
            right = jnp.concatenate([spread(value, masks), ones], axis=1)
            state[unit] = nn(state[unit], right)[:PAD]

        def finish(unit):
            window, group = divmod(unit, GROUPS)
            at = group * LANES
            both = state[unit]
            rows = pl.ds(pl.multiple_of(image * PIC + window * PAD, 8), PAD)
            att_ref[rows, at : at + LANES] = (both[:, :LANES] / both[:, LANES:]).astype(bf16)
            state[unit] = None

        begin(0)
        begin(1)
        for unit in range(units):
            soften(unit)
            mix(unit)
            if unit + 2 < units:
                begin(unit + 2)
            if unit > 0:
                finish(unit - 1)
        finish(units - 1)
        return carry

    lax.fori_loop(0, pics, image_step, 0)


def middle(
    owners, used, own_ref, recv_ref, xw_ref, att_ref, perm_ref, back_ref, vec_ref, upb_ref,
    *rest, shards, pics
):
    wo_refs, w1_refs, w2_refs = rest[:shards], rest[shards : 2 * shards], rest[2 * shards : 3 * shards]
    (
        keep_ref, send_ref, resid_ref, datt_ref, gkeep_ref, gsend_ref, vecg_ref, upg_ref,
        wo, w1, w2, stage, n2s, cts, gn2s, mlps, acc1, acc2, acco, sems,
    ) = rest[3 * shards :]
    step = pl.program_id(0)
    last = pl.num_programs(0) - 1

    @pl.when(step == 0)
    def _():
        copies = (
            load_shards(owners, wo_refs, wo, sems.at[0])
            + load_shards(owners, w1_refs, w1, sems.at[1])
            + load_shards(owners, w2_refs, w2, sems.at[2])
        )
        for copy in copies:
            copy.start()
        stage[...] = jnp.zeros_like(stage)
        acc1[...] = jnp.zeros_like(acc1)
        acc2[...] = jnp.zeros_like(acc2)
        acco[...] = jnp.zeros_like(acco)
        vecg_ref[...] = jnp.zeros_like(vecg_ref)
        upg_ref[...] = jnp.zeros_like(upg_ref)
        for copy in copies:
            copy.wait()

    perm = perm_ref[...]
    back = back_ref[...]
    pbias = vec_ref[4:5]
    gain = vec_ref[5:6]
    beta = vec_ref[6:7]
    dbias = vec_ref[7:8]
    for image in range(pics):
        stage_rows(stage, own_ref, recv_ref, image)
        flag = used[step * pics + image].astype(f32)
        rows = pl.ds(image * PIC, PIC)
        cts[rows] = (to_windows(stage, perm, image) * flag).astype(bf16)
    proj = (nn(att_ref[...], wo[...]) + pbias).astype(bf16)
    resid = xw_ref[...].astype(f32) + proj.astype(f32)
    hat, rstd = stats(resid)
    n2s[...] = (hat * gain + beta).astype(bf16)
    mlps[...] = resid + dbias
    gn2s[...] = jnp.zeros_like(gn2s)
    n2t = n2s[...].T
    ctt = cts[...].T
    span = w1.shape[1] // 4

    def chunk(index, carry):
        cols = pl.ds(pl.multiple_of(index * span, span), span)
        pre = nn(n2s[...], w1[:, cols]) + upb_ref[0:1, cols]
        dact = nt(cts[...], w2[cols, :])
        phi = 0.5 * (1.0 + lax.erf(pre * 0.7071067811865476))
        act = (pre * phi).astype(bf16)
        slope = phi + pre * jnp.exp(-0.5 * pre * pre) * 0.3989422804014327
        gpre = dact * slope
        upg_ref[0:1, cols] += rowsum(gpre)
        hidden = gpre.astype(bf16)
        mlps[...] += nn(act, w2[cols, :])
        gn2s[...] += nt(hidden, w1[:, cols])
        acc2[:, cols] += nn(ctt, act)
        acc1[:, cols] += nn(n2t, hidden)
        return carry

    lax.fori_loop(0, 4, chunk, 0)

    gn2 = gn2s[...]
    ct = cts[...].astype(f32)
    gresid = ct + norm_back(gn2 * gain, hat, rstd)
    vecg_ref[4:5] += rowsum(gresid)
    vecg_ref[5:6] += rowsum(gn2 * hat)
    vecg_ref[6:7] += rowsum(gn2)
    vecg_ref[7:8] += rowsum(ct)
    low = gresid.astype(bf16)
    resid_ref[...] = low
    datt = nt(low, wo[...])
    for window in range(2 * pics):
        datt_ref[window, :PAD] = datt[window * PAD : (window + 1) * PAD].astype(bf16)
        datt_ref[window, PAD:] = jnp.zeros((SEG - PAD, D), bf16)
    acco[...] += tn(att_ref[...], low)
    for image in range(pics):
        flag = used[step * pics + image].astype(f32)
        rows = pl.ds(image * PIC, PIC)
        mine = (mlps[rows] * flag).astype(bf16)
        framed = nn(back, mine).astype(bf16).reshape(WIN, COLS, D)
        for row in range(OWN):
            keep_ref[image, row] = framed[row, :SIDE]
        for row in range(SHIFT):
            send_ref[image, row] = framed[OWN + row, :SIDE]

    @pl.when(step == last)
    def _():
        count = D // shards
        tall = w2.shape[0] // shards
        for pair in range(shards // 2):
            for target, flip in ((gkeep_ref, 0), (gsend_ref, 1)):
                place = 2 * pair + ((owners[0] & 1) ^ flip)
                rows = pl.ds(pl.multiple_of(place * count, count), count)
                for piece in range(4):
                    target[pair, piece * count : (piece + 1) * count] = acc1[
                        rows, piece * span : (piece + 1) * span
                    ].astype(bf16)
                cols = pl.ds(pl.multiple_of(place * tall, tall), tall)
                target[pair, 4 * count : 4 * count + tall] = acc2[:, cols].T.astype(bf16)
                target[pair, 4 * count + tall :] = acco[rows].astype(bf16)


def backward_attention(
    qkv_ref, datt_ref, table_ref, sum_in_ref, tab_in_ref, *rest, pics, chained
):
    dqkv_ref, sum_ref, tab_ref = rest[1 if chained else 0 :]

    @pl.when(pl.program_id(0) == 0)
    def _():
        sum_ref[...] = sum_in_ref[...]
        tab_ref[...] = tab_in_ref[...]

    masks = head_masks(bf16)
    picks = head_masks(f32)
    units = 2 * GROUPS

    def fold(values):
        return jnp.sum(values.reshape(PAD // 8, 8, LANES), 0)

    def image_step(image, carry):
        state = [None] * units

        def begin(unit):
            window, group = divmod(unit, GROUPS)
            at = group * LANES
            place = image * 2 + window
            query = qkv_ref[place, :, at : at + LANES]
            key = qkv_ref[place, :, D + at : D + at + LANES]
            value = qkv_ref[place, :, 2 * D + at : 2 * D + at + LANES]
            queries = spread(query, masks)
            datts = spread(datt_ref[place, :, at : at + LANES], masks)
            state[unit] = (nt(key, queries)[:PAD], nt(value, datts)[:PAD])

        def soften(unit):
            window, group = divmod(unit, GROUPS)
            raw, dprobs = state[unit]
            scores = raw + table_ref[window, group]
            shifted = jnp.exp(scores - jnp.max(scores, 0, keepdims=True))
            probs = shifted * (1.0 / jnp.sum(shifted, 0, keepdims=True))
            inner = jnp.sum(probs * dprobs, 0, keepdims=True)
            dscores = probs * (dprobs - inner)
            tab_ref[group] += dscores
            state[unit] = (pad_rows(dscores).astype(bf16), pad_rows(probs).astype(bf16))

        def mix(unit):
            window, group = divmod(unit, GROUPS)
            at = group * LANES
            place = image * 2 + window
            dlow, plow = state[unit]
            query = qkv_ref[place, :, at : at + LANES]
            key = qkv_ref[place, :, D + at : D + at + LANES]
            dkey = nn(dlow, spread(query, masks))[:PAD]
            dvalue = nn(plow, spread(datt_ref[place, :, at : at + LANES], masks))[:PAD]
            state[unit] = (dkey, dvalue, tn(dlow, key))

        def finish(unit):
            window, group = divmod(unit, GROUPS)
            at = group * LANES
            dkey, dvalue, tall = state[unit]
            dquery = tall[0:PAD] * picks[0][:PAD]
            for head in range(1, QUAD):
                dquery += tall[head * SEG : head * SEG + PAD] * picks[head][:PAD]
            dquery = dquery * SCALE
            rows = pl.ds(pl.multiple_of(image * PIC + window * PAD, 8), PAD)
            dqkv_ref[rows, at : at + LANES] = dquery.astype(bf16)
            dqkv_ref[rows, D + at : D + at + LANES] = dkey.astype(bf16)
            dqkv_ref[rows, 2 * D + at : 2 * D + at + LANES] = dvalue.astype(bf16)
            sum_ref[0, :, at : at + LANES] += fold(dquery)
            sum_ref[1, :, at : at + LANES] += fold(dvalue)
            state[unit] = None

        begin(0)
        begin(1)
        for unit in range(units):
            soften(unit)
            mix(unit)
            if unit + 2 < units:
                begin(unit + 2)
            if unit > 0:
                finish(unit - 1)
        finish(units - 1)
        return carry

    lax.fori_loop(0, pics, image_step, 0)


def weight_grad(owners, xw_ref, dqkv_ref, vec_ref, gkeep_ref, gsend_ref, acc, *, shards):
    @pl.when(pl.program_id(0) == 0)
    def _():
        acc[...] = jnp.zeros_like(acc)

    hat, _ = stats(xw_ref[...].astype(f32))
    normed = (hat * vec_ref[0:1] + vec_ref[1:2]).astype(bf16)
    acc[...] += tn(normed, dqkv_ref[...])

    @pl.when(pl.program_id(0) == pl.num_programs(0) - 1)
    def _():
        count = D // shards
        for pair in range(shards // 2):
            for target, flip in ((gkeep_ref, 0), (gsend_ref, 1)):
                place = 2 * pair + ((owners[0] & 1) ^ flip)
                rows = pl.ds(pl.multiple_of(place * count, count), count)
                target[pair] = acc[rows].astype(bf16)


def input_grad(
    owners, xw_ref, dqkv_ref, resid_ref, back_ref, vec_ref, sum_in_ref, *rest, shards, pics, chained
):
    weight_refs = rest[:shards]
    keep_ref, send_ref, vecg_ref, weight, sems = rest[shards + (1 if chained else 0) :]

    @pl.when(pl.program_id(0) == 0)
    def _():
        copies = load_shards(owners, weight_refs, weight, sems)
        for copy in copies:
            copy.start()
        vecg_ref[...] = sum_in_ref[...]
        for copy in copies:
            copy.wait()

    gain = vec_ref[0:1]
    hat, rstd = stats(xw_ref[...].astype(f32))
    gnormed = nt(dqkv_ref[...], weight[...]).astype(bf16).astype(f32)
    vecg_ref[0:1] += rowsum(gnormed * hat)
    vecg_ref[1:2] += rowsum(gnormed)
    ginput = resid_ref[...].astype(f32) + norm_back(gnormed * gain, hat, rstd)
    glow = ginput.astype(bf16)
    back = back_ref[...]
    for image in range(pics):
        framed = nn(back, glow[image * PIC : (image + 1) * PIC]).astype(bf16).reshape(WIN, COLS, D)
        for row in range(OWN):
            keep_ref[image, row] = framed[row, :SIDE]
        for row in range(SHIFT):
            send_ref[image, row] = framed[OWN + row, :SIDE]


def pack_small(*refs, count, span):
    rows_ref = refs[-1]
    up_ref, table_ref = refs[-3], refs[-2]
    rows_ref[...] = jnp.zeros_like(rows_ref)
    for at in range(count):
        rows_ref[at : at + 1, : refs[at].shape[1]] = refs[at][...].astype(f32)
    at = count
    for piece in range(up_ref.shape[1] // span):
        rows_ref[at : at + 1] = up_ref[:, piece * span : (piece + 1) * span].astype(f32)
        at += 1
    rows_ref[at : at + table_ref.shape[0], : table_ref.shape[1]] = table_ref[...].astype(f32)


def tie(value, *others):
    return lax.optimization_barrier((value, *others))[0]


class Reduction:
    def __init__(self, keep, send):
        self.keep = keep
        self.send = send
        self.exchange("fsdp", 0)
        img = list(range(bits_of("img")))
        self.plan = (
            [("pick", "fsdp", bit) for bit in range(1, bits_of("fsdp"))]
            + [("halve", "img", bit) for bit in img]
            + [("full", "band", bit) for bit in range(bits_of("band"))]
            + [("join", "img", bit) for bit in reversed(img)]
        )
        self.joined = None

    def total(self):
        if self.joined is None:
            return (self.keep.astype(f32) + self.got.astype(f32)).astype(bf16)
        first = jnp.concatenate([self.keep, self.got], axis=0)
        second = jnp.concatenate([self.got, self.keep], axis=0)
        return jnp.where(self.joined == 0, first, second)

    def advance(self):
        total = self.total()
        kind, axis, bit = self.plan.pop(0)
        mine = (lax.axis_index(axis) >> bit) & 1
        self.joined = None
        if kind == "pick":
            total = total.reshape(total.shape[0] // 2, 2, *total.shape[1:])
            self.keep = lax.dynamic_index_in_dim(total, mine, 1, keepdims=False)
            self.send = lax.dynamic_index_in_dim(total, 1 - mine, 1, keepdims=False)
        elif kind == "halve":
            total = total.reshape(2, total.shape[-2] // 2, total.shape[-1])
            self.keep = lax.dynamic_index_in_dim(total, mine, 0, keepdims=False)
            self.send = lax.dynamic_index_in_dim(total, 1 - mine, 0, keepdims=False)
        else:
            self.keep = self.send = total
            if kind == "join":
                self.joined = mine
        self.exchange(axis, bit)
        return self.send

    def exchange(self, axis, bit):
        self.got = partner(self.send, axis, bit)

    def settle(self, value):
        self.got = tie(self.got, value)
        return self.total()[0]

    def advance_after(self, value):
        self.got = tie(self.got, value)
        return self.advance()

    def finish(self):
        while self.plan:
            self.advance()
        return self.total()


def gather(piece):
    held = [piece]
    for bit in reversed(range(bits_of("fsdp"))):
        held = held + [partner(one, "fsdp", bit) for one in held]
    return held


def held_masks():
    masks = [0]
    for bit in reversed(range(bits_of("fsdp"))):
        masks = masks + [mask | (1 << bit) for mask in masks]
    return masks


def in_order(held, me):
    masks = held_masks()
    count = len(held)
    table = [None] * count
    for mask, piece in zip(masks, held):
        table[mask] = piece
    stacked = jnp.stack(table)
    for bit in range(bits_of("fsdp")):
        split = stacked.reshape(count >> (bit + 1), 2, 1 << bit, *stacked.shape[1:])
        swap = (me >> bit) & 1
        split = jnp.where(swap == 1, split[:, ::-1], split)
        stacked = split.reshape(stacked.shape)
    return stacked


def window_tables():
    rows, cols = np.arange(PAD)[:, None], np.arange(SEG)[None, :]
    real = (rows < LEN) & (cols < LEN)

    def index(one, other):
        at = (one // WIN - other // WIN + WIN - 1) * (2 * WIN - 1) + one % WIN - other % WIN + WIN - 1
        return np.where(real, at, TABLE)

    places = jnp.asarray(np.stack([index(rows, cols), index(cols, rows)]), jnp.int32)
    hots = lax.optimization_barrier(places)[..., None] == jnp.arange(TABLE)
    cells = np.arange(SIDE)
    region = np.where(cells < SIDE - WIN, 0, np.where(cells < SIDE - SHIFT, 1, 2))
    split = region.reshape(SIDE // WIN, WIN)
    label = (split[:, None, :, None] * 3 + split[None, :, None, :]).reshape(2, 2, LEN)
    wide = np.pad(label, ((0, 0), (0, 0), (0, SEG - LEN)), constant_values=-1)
    differ = wide[..., :PAD, None] != wide[..., None, :]
    forward = differ | (cols >= LEN)
    backward = (differ & (cols < LEN)) | (rows >= LEN)
    blocks = np.where(np.stack([forward, backward]), NEGATIVE, 0.0)
    return hots.astype(bf16), jnp.asarray(blocks, f32)


def block_pass(
    block_input,
    slot_used,
    cotangent,
    ln1_gain,
    ln1_bias,
    w_qkv,
    q_bias,
    v_bias,
    rel_table,
    w_out,
    out_bias,
    ln2_gain,
    ln2_bias,
    w_fc1,
    fc1_bias,
    w_fc2,
    fc2_bias,
):
    slots = block_input.shape[0]
    ranks = lax.axis_size("fsdp")
    width = w_fc1.shape[1]
    me = lax.axis_index("fsdp")
    band = lax.axis_index("band")
    owners = jnp.stack([me ^ mask for mask in held_masks()]).astype(jnp.int32)
    third = slots // 3
    total = slots * PIC

    any_spec = pl.BlockSpec(memory_space=pl.ANY)

    def whole(shape):
        return pl.BlockSpec(shape, lambda i, *_: (0,) * len(shape))

    def block(shape, base=0):
        return pl.BlockSpec(shape, lambda i, *_: (i + base,) + (0,) * (len(shape) - 1))

    def like(shape, dtype):
        return jax.ShapeDtypeStruct(shape, dtype)

    params = pltpu.CompilerParams(
        dimension_semantics=("arbitrary",), vmem_limit_bytes=60 * 1024 * 1024
    )

    def call(kernel, micros, grid, prefetch, in_specs, out_specs, out_shape, scratch, aliases={}):
        cost = pl.CostEstimate(
            flops=int(micros * MICRO_FLOPS), bytes_accessed=int(micros * MICRO_BYTES), transcendentals=0
        )
        return pl.pallas_call(
            kernel,
            grid_spec=pltpu.PrefetchScalarGridSpec(
                num_scalar_prefetch=prefetch,
                grid=(grid,),
                in_specs=in_specs,
                out_specs=out_specs,
                scratch_shapes=scratch,
            ),
            out_shape=out_shape,
            input_output_aliases=aliases,
            compiler_params=params,
            cost_estimate=cost,
        )

    arrivals = []
    for piece in range(3):
        edge = block_input[piece * third : (piece + 1) * third, :SHIFT]
        arrivals.append(partner(edge, "band", 0))
    held_qkv = gather(w_qkv)

    per = ln1_gain.shape[0]
    ups = fc1_bias.shape[0]
    heads = rel_table.shape[0]
    span = 2 * LANES
    vectors8 = (ln1_gain, ln1_bias, q_bias, v_bias, out_bias, ln2_gain, ln2_bias, fc2_bias)
    lines = -(-(8 + ups // span + heads) // 8) * 8
    packed = pl.pallas_call(
        functools.partial(pack_small, count=8, span=span),
        out_shape=like((lines, span), f32),
        name="pack_small",
    )(*[one.reshape(1, -1) for one in vectors8], fc1_bias.reshape(1, -1), rel_table)
    held_small = gather(packed)
    small = in_order(held_small, me)
    vectors = small[:, :8, :per].transpose(1, 0, 2).reshape(8, D)
    up_bias = small[:, 8 : 8 + ups // span].reshape(1, width)
    table = small[:, 8 + ups // span : 8 + ups // span + heads, :TABLE].reshape(HEADS, TABLE).astype(bf16)

    hots, blocks = window_tables()
    quads = table.reshape(GROUPS, QUAD, TABLE)
    biases = jnp.einsum("ght,zijt->zgihj", quads, hots, preferred_element_type=f32)
    masks = lax.dynamic_index_in_dim(blocks, band, 1, keepdims=False)
    table_f, table_b = (
        (biases[at][None] + masks[at][:, None, :, None, :]).reshape(2, GROUPS, PAD, QUAD * SEG)
        for at in range(2)
    )
    two = hots[1]

    target = np.arange(PIC)
    window, spot_in = target // PAD, target % PAD
    source = (spot_in // WIN) * COLS + (window * WIN + spot_in % WIN + SHIFT) % SIDE
    source = np.where(spot_in < LEN, source, -1)
    perm = jnp.asarray(source[:, None] == np.arange(WIN * COLS)[None, :], bf16)
    back = jnp.asarray(source[None, :] == np.arange(WIN * COLS)[:, None], bf16)

    first = lax.optimization_barrier((w_out, w_fc1, w_fc2, held_qkv[-1], held_small[-1]))[:3]
    held_late = [[one] for one in first]
    far = bits_of("fsdp") - 1
    for held in held_late:
        held.append(partner(held[0], "fsdp", far))

    pics = 4
    rows = pics * PIC
    table_shape = (2, GROUPS, PAD, QUAD * SEG)
    state = None
    for piece in range(3):
        steps = third // pics
        base = piece * steps
        if piece == 2:
            sends = [held[-1] for held in held_late]
            tied = lax.optimization_barrier((arrivals[piece], state[0], *sends))
            arrivals[piece] = tied[0]
            for held, sent in zip(held_late, tied[2:]):
                held[-1] = sent
                for bit in reversed(range(far)):
                    held.extend([partner(part, "fsdp", bit) for part in held])
        chained = state is not None
        state = call(
            functools.partial(forward_attention, shards=ranks, pics=pics, chained=chained),
            1.6 * third,
            steps,
            1,
            [
                block((pics, WIN, SIDE, D), base), block((pics, SHIFT, SIDE, D)), whole((PIC, PIC)),
                whole((8, D)), whole(table_shape),
            ] + [any_spec] * (ranks + (3 if chained else 0)),
            [block((rows, D), base), block((2 * pics, SEG, 3 * D), base), block((rows, D), base)],
            [like((total, D), bf16), like((2 * slots, SEG, 3 * D), bf16), like((total, D), bf16)],
            [
                pltpu.VMEM((D, 3 * D), bf16),
                pltpu.VMEM((pics, WIN, COLS, D), bf16),
                pltpu.VMEM((rows, D), bf16),
                pltpu.SemaphoreType.DMA((ranks,)),
            ],
            {6 + ranks + at: at for at in range(3)} if chained else {},
        )(
            owners, block_input, arrivals[piece], perm, vectors, table_f, *held_qkv,
            *(state if chained else ()),
        )
        if piece == 0:
            cotangent = tie(cotangent, state[0])
            ct_arrived = partner(cotangent[:, :SHIFT], "band", 0)
    xw, qkv, att = state
    held_out, held_up, held_down = held_late

    pack = D // ranks * (width // D) + width // ranks + D // ranks
    half = ranks // 2
    keep, send, resid, datt, gkeep, gsend, vecg, upg = call(
        functools.partial(middle, shards=ranks, pics=pics),
        2.7 * slots,
        slots // pics,
        2,
        [
            block((pics, WIN, SIDE, D)), block((pics, SHIFT, SIDE, D)), block((rows, D)), block((rows, D)),
            whole((PIC, PIC)), whole((PIC, PIC)), whole((8, D)), whole((1, width)),
        ] + [any_spec] * (3 * ranks),
        [
            block((pics, OWN, SIDE, D)), block((pics, SHIFT, SIDE, D)), block((rows, D)),
            block((2 * pics, SEG, D)), whole((half, pack, D)), whole((half, pack, D)),
            whole((8, D)), whole((1, width)),
        ],
        [
            like((slots, OWN, SIDE, D), bf16), like((slots, SHIFT, SIDE, D), bf16),
            like((total, D), bf16), like((2 * slots, SEG, D), bf16), like((half, pack, D), bf16),
            like((half, pack, D), bf16), like((8, D), f32), like((1, width), f32),
        ],
        [
            pltpu.VMEM((D, D), bf16),
            pltpu.VMEM((D, width), bf16),
            pltpu.VMEM((width, D), bf16),
            pltpu.VMEM((pics, WIN, COLS, D), bf16),
            pltpu.VMEM((rows, D), bf16),
            pltpu.VMEM((rows, D), bf16),
            pltpu.VMEM((rows, D), f32),
            pltpu.VMEM((rows, D), f32),
            pltpu.VMEM((D, width), f32),
            pltpu.VMEM((D, width), f32),
            pltpu.VMEM((D, D), f32),
            pltpu.SemaphoreType.DMA((3, ranks)),
        ],
    )(
        owners, slot_used.reshape(-1), cotangent, ct_arrived, xw, att, perm, back, vectors, up_bias,
        *held_out, *held_up, *held_down,
    )

    mlp = Reduction(gkeep, gsend)
    returned = partner(send, "band", 0)
    pics = 2
    rows = pics * PIC
    steps = slots // pics
    unit = steps // 6
    sums = jnp.zeros((2, 8, D), f32)
    tab = jnp.zeros((GROUPS, PAD, QUAD * SEG), f32)
    lnsum = jnp.zeros((8, D), f32)
    dqkv = gin = None
    gparts = []

    def attend_part(base, count, tab, sums, dqkv, token):
        chained = dqkv is not None
        if token is not None:
            sums = tie(sums, token)
        return call(
            functools.partial(backward_attention, pics=pics, chained=chained),
            1.9 * 2 * count,
            count,
            0,
            [
                block((2 * pics, SEG, 3 * D), base), block((2 * pics, SEG, D), base),
                whole(table_shape), whole((2, 8, D)), whole((GROUPS, PAD, QUAD * SEG)),
            ] + [any_spec] * chained,
            [block((rows, 3 * D), base), whole((2, 8, D)), whole((GROUPS, PAD, QUAD * SEG))],
            [
                like((total, 3 * D), bf16), like((2, 8, D), f32),
                like((GROUPS, PAD, QUAD * SEG), f32),
            ],
            [],
            {5: 0} if chained else {},
        )(qkv, datt, table_b, sums, tab, *((dqkv,) if chained else ()))

    def descend_part(first, count, lnsum, gin, token):
        images = 4
        tall = images * PIC
        base = first // images
        chained = gin is not None
        if token is not None:
            lnsum = tie(lnsum, token)
        return call(
            functools.partial(input_grad, shards=ranks, pics=images, chained=chained),
            0.8 * count,
            count // images,
            1,
            [
                block((tall, D), base), block((tall, 3 * D), base), block((tall, D), base),
                whole((PIC, PIC)), whole((8, D)), whole((8, D)),
            ] + [any_spec] * (ranks + chained),
            [block((images, OWN, SIDE, D), base), block((images, SHIFT, SIDE, D)), whole((8, D))],
            [
                like((slots, OWN, SIDE, D), bf16), like((count, SHIFT, SIDE, D), bf16),
                like((8, D), f32),
            ],
            [pltpu.VMEM((D, 3 * D), bf16), pltpu.SemaphoreType.DMA((ranks,))],
            {7 + ranks: 0} if chained else {},
        )(
            owners, xw, dqkv, resid, back, vectors, lnsum, *held_qkv, *((gin,) if chained else ()),
        )

    dqkv, sums, tab = attend_part(0, unit, tab, sums, dqkv, None)
    token = mlp.advance_after(sums)
    dqkv, sums, tab = attend_part(unit, 2 * unit, tab, sums, dqkv, token)
    early = 3 * unit * pics
    gin, gpart, lnsum = descend_part(0, early, lnsum, gin, None)
    gparts.append(partner(gpart, "band", 0))
    token = mlp.advance_after(lnsum)
    dqkv, sums, tab = attend_part(3 * unit, 2 * unit, tab, sums, dqkv, token)
    token = mlp.advance_after(sums)
    dqkv, sums, tab = attend_part(5 * unit, steps - 5 * unit, tab, sums, dqkv, token)

    images = 8
    tall = images * PIC
    qkeep, qsend = call(
        functools.partial(weight_grad, shards=ranks),
        0.49 * slots,
        slots // images,
        1,
        [block((tall, D)), block((tall, 3 * D)), whole((8, D))],
        [whole((half, D // ranks, 3 * D)), whole((half, D // ranks, 3 * D))],
        [like((half, D // ranks, 3 * D), bf16), like((half, D // ranks, 3 * D), bf16)],
        [pltpu.VMEM((D, 3 * D), f32)],
    )(owners, xw, dqkv, vectors)
    token = mlp.advance_after(qkeep)
    own = Reduction(qkeep, qsend)
    gin, gpart, lnsum = descend_part(early, slots - early, lnsum, gin, token)
    gparts.append(partner(gpart, "band", 0))
    mlp.advance_after(lnsum)

    count = D // ranks
    lanes = width // D
    spots = tab.reshape(GROUPS, PAD, QUAD, SEG)
    high = lax.reduce_precision(spots, 8, 7)
    both = jnp.stack([high, spots - high]).astype(bf16)
    grad_table = jnp.einsum("zgihj,ijt->ght", both, two, preferred_element_type=f32)
    flat = jnp.concatenate([
        lnsum[:2], jnp.sum(sums, 1), vecg[4:], upg.reshape(-1, D),
        jnp.pad(grad_table.reshape(HEADS, TABLE), ((0, 0), (0, D - TABLE))),
    ])
    own.advance()
    swaps = [(axis, bit) for axis in ("fsdp", "band", "img") for bit in range(bits_of(axis))]
    stage = 0
    while own.plan or swaps:
        token = own.got
        if swaps:
            got = partner(flat, *swaps.pop(0))
            flat, token = lax.optimization_barrier((flat + got, token))
        if stage == 1:
            token = tie(token, gparts[1])
        own.got = token
        if own.plan:
            own.advance()
        stage += 1
    mine = lax.dynamic_index_in_dim(flat[:8].reshape(8, ranks, per), me, 1, keepdims=False)
    own_upb = lax.dynamic_slice_in_dim(flat[8 : 8 + lanes].reshape(-1), me * ups, ups)
    own_table = lax.dynamic_slice_in_dim(flat, 8 + lanes + me * heads, heads)[:, :TABLE]
    packed = mlp.finish().astype(f32)
    own_up = packed[: lanes * count].reshape(lanes, count, D).transpose(1, 0, 2).reshape(count, width)
    own_down = packed[lanes * count : lanes * count + width // ranks]
    own_out = packed[lanes * count + width // ranks :]

    own_qkv = own.finish().astype(f32)

    output = jnp.concatenate([returned, keep], axis=1)
    grad_input = jnp.concatenate([jnp.concatenate(gparts, axis=0), gin], axis=1).astype(f32)
    return (
        output,
        grad_input,
        mine[0],
        mine[1],
        own_qkv,
        mine[2],
        mine[3],
        own_table,
        own_out,
        mine[4],
        mine[5],
        mine[6],
        own_up,
        own_upb,
        own_down,
        mine[7],
    )


def solution(mesh):
    pictures = P(("img", "fsdp"), "band", None, None)
    flat = P("fsdp")
    wide = P("fsdp", None)
    return jax.shard_map(
        block_pass,
        mesh=mesh,
        in_specs=(
            pictures, P(("img", "fsdp"), None), pictures, flat, flat, wide, flat, flat, wide, wide,
            flat, flat, flat, wide, flat, wide, flat,
        ),
        out_specs=(
            pictures, pictures, flat, flat, wide, flat, flat, wide, wide, flat, flat, flat, wide,
            flat, wide, flat,
        ),
        check_vma=False,
    )
```

```python
import functools

import jax
import jax.numpy as jnp
import numpy as np
from jax import lax
from jax.experimental import pallas as pl
from jax.experimental.pallas import tpu as pltpu
from jax.sharding import PartitionSpec as P


D = 512
HEADS = 16
WIN = 7
SHIFT = 3
SIDE = 14
TABLE = 169
LEN = WIN * WIN
EPSILON = 1e-05
NEGATIVE = -1e30

PAD = 56
SEG = 64
PIC = 2 * PAD
COLS = 16
QUAD = 4
GROUPS = HEADS // QUAD
LANES = 128
HEAD = D // HEADS
SCALE = HEAD ** (-0.5)
OWN = WIN - SHIFT

MICRO_FLOPS = 1.15e9
MICRO_BYTES = 3.0e6

f32 = jnp.float32
bf16 = jnp.bfloat16


def partner(value, axis, bit):
    mask = 1 << bit
    pairs = [(source, source ^ mask) for source in range(lax.axis_size(axis))]
    return lax.ppermute(value, axis, pairs)


def bits_of(axis):
    return (lax.axis_size(axis) - 1).bit_length()


def nt(left, right):
    return lax.dot_general(left, right, (((1,), (1,)), ((), ())), preferred_element_type=f32)


def nn(left, right):
    return jnp.dot(left, right, preferred_element_type=f32)


def tn(left, right):
    return lax.dot_general(left, right, (((0,), (0,)), ((), ())), preferred_element_type=f32)


def stats(values):
    center = values - jnp.mean(values, -1, keepdims=True)
    rstd = lax.rsqrt(jnp.mean(center * center, -1, keepdims=True) + EPSILON)
    return center * rstd, rstd


def norm_back(grad_hat, normal, rstd):
    return rstd * (
        grad_hat
        - jnp.mean(grad_hat, -1, keepdims=True)
        - normal * jnp.mean(grad_hat * normal, -1, keepdims=True)
    )


def rowsum(values):
    return jnp.sum(values, 0, keepdims=True)


def load_shards(owners, refs, target, sems):
    rows = refs[0].shape[0]
    copies = []
    for at, ref in enumerate(refs):
        start = pl.multiple_of(owners[at] * rows, rows)
        copies.append(pltpu.make_async_copy(ref, target.at[pl.ds(start, rows)], sems.at[at]))
    return copies


def stage_rows(stage, own_ref, recv_ref, image):
    for row in range(OWN):
        stage[image, row, :SIDE, :] = own_ref[image, SHIFT + row]
    for row in range(SHIFT):
        stage[image, OWN + row, :SIDE, :] = recv_ref[image, row]


def to_windows(stage, perm, image):
    flat = stage[image].reshape(WIN * COLS, D)
    return nn(perm, flat)


def pad_rows(values):
    return jnp.concatenate([values, jnp.zeros((SEG - PAD, values.shape[1]), f32)], axis=0)


def head_masks(dtype):
    lane = lax.broadcasted_iota(jnp.int32, (SEG, LANES), 1) // HEAD
    return [jnp.where(lane == head, 1.0, 0.0).astype(dtype) for head in range(QUAD)]


def spread(block, masks):
    return jnp.concatenate([block * mask for mask in masks], axis=0)


def clear(ref):
    rows = ref.shape[0] // 8

    def each(block, carry):
        part = pl.ds(pl.multiple_of(block * rows, rows), rows)
        ref[part] = jnp.zeros((rows, *ref.shape[1:]), ref.dtype)
        return carry

    lax.fori_loop(0, 8, each, 0)


def forward_attention(
    owners, own_ref, recv_ref, perm_ref, vec_ref, table_ref, *rest, shards, pics, chained
):
    weight_refs = rest[:shards]
    rest = rest[shards + (3 if chained else 0) :]
    xw_ref, qkv_ref, att_ref, weight, stage, norms, sems = rest

    @pl.when(pl.program_id(0) == 0)
    def _():
        copies = load_shards(owners, weight_refs, weight, sems)
        for copy in copies:
            copy.start()
        stage[...] = jnp.zeros_like(stage)
        for copy in copies:
            copy.wait()

    perm = perm_ref[...]
    gain = vec_ref[0:1]
    beta = vec_ref[1:2]
    for image in range(pics):
        stage_rows(stage, own_ref, recv_ref, image)
        values = to_windows(stage, perm, image)
        rows = pl.ds(image * PIC, PIC)
        xw_ref[rows] = values.astype(bf16)
        hat, _ = stats(values)
        norms[rows] = (hat * gain + beta).astype(bf16)
    normed = norms[...]
    for part in range(3):
        product = nn(normed, weight[:, part * D : (part + 1) * D])
        if part == 0:
            product = (product + vec_ref[2:3]) * SCALE
        if part == 2:
            product = product + vec_ref[3:4]
        for window in range(2 * pics):
            qkv_ref[window, :PAD, part * D : (part + 1) * D] = product[
                window * PAD : (window + 1) * PAD
            ].astype(bf16)
    for window in range(2 * pics):
        qkv_ref[window, PAD:] = jnp.zeros((SEG - PAD, 3 * D), bf16)

    masks = head_masks(bf16)
    half = lax.broadcasted_iota(jnp.int32, (PAD, LANES), 1) < SEG
    row_head = lax.broadcasted_iota(jnp.int32, (QUAD * SEG, LANES), 0) // SEG
    lane_head = lax.broadcasted_iota(jnp.int32, (QUAD * SEG, LANES), 1) // HEAD
    ones = jnp.where(row_head == lane_head, 1.0, 0.0).astype(bf16)
    units = 2 * GROUPS

    def image_step(image, carry):
        state = [None] * units

        def begin(unit):
            window, group = divmod(unit, GROUPS)
            at = group * LANES
            place = image * 2 + window
            query = qkv_ref[place, :, at : at + LANES]
            key = qkv_ref[place, :, D + at : D + at + LANES]
            state[unit] = nt(query, spread(key, masks))[:PAD]

        def soften(unit):
            window, group = divmod(unit, GROUPS)
            scores = state[unit] + table_ref[window, group]
            parts = []
            for side in range(2):
                block = scores[:, side * LANES : (side + 1) * LANES]
                low = jnp.max(jnp.where(half, block, NEGATIVE), -1, keepdims=True)
                high = jnp.max(jnp.where(half, NEGATIVE, block), -1, keepdims=True)
                parts.append(jnp.exp(block - jnp.where(half, low, high)))
            state[unit] = pad_rows(jnp.concatenate(parts, axis=1)).astype(bf16)

        def mix(unit):
            window, group = divmod(unit, GROUPS)
            at = group * LANES
            value = qkv_ref[image * 2 + window, :, 2 * D + at : 2 * D + at + LANES]
            right = jnp.concatenate([spread(value, masks), ones], axis=1)
            state[unit] = nn(state[unit], right)[:PAD]

        def finish(unit):
            window, group = divmod(unit, GROUPS)
            at = group * LANES
            both = state[unit]
            rows = pl.ds(pl.multiple_of(image * PIC + window * PAD, 8), PAD)
            att_ref[rows, at : at + LANES] = (both[:, :LANES] / both[:, LANES:]).astype(bf16)
            state[unit] = None

        begin(0)
        begin(1)
        for unit in range(units):
            soften(unit)
            mix(unit)
            if unit + 2 < units:
                begin(unit + 2)
            if unit > 0:
                finish(unit - 1)
        finish(units - 1)
        return carry

    lax.fori_loop(0, pics, image_step, 0)


def middle(
    owners, used, own_ref, recv_ref, xw_ref, att_ref, perm_ref, back_ref, vec_ref, upb_ref,
    *rest, shards, pics
):
    wo_refs, w1_refs, w2_refs = rest[:shards], rest[shards : 2 * shards], rest[2 * shards : 3 * shards]
    (
        keep_ref, send_ref, resid_ref, datt_ref, gkeep_ref, gsend_ref, vecg_ref, upg_ref,
        wo, w1, w2, stage, n2s, cts, gn2s, mlps, acc1, acc2, acco, sems,
    ) = rest[3 * shards :]
    step = pl.program_id(0)
    last = pl.num_programs(0) - 1

    @pl.when(step == 0)
    def _():
        copies = (
            load_shards(owners, wo_refs, wo, sems.at[0])
            + load_shards(owners, w1_refs, w1, sems.at[1])
            + load_shards(owners, w2_refs, w2, sems.at[2])
        )
        for copy in copies:
            copy.start()
        stage[...] = jnp.zeros_like(stage)
        clear(acc1)
        clear(acc2)
        clear(acco)
        vecg_ref[...] = jnp.zeros_like(vecg_ref)
        upg_ref[...] = jnp.zeros_like(upg_ref)
        for copy in copies:
            copy.wait()

    perm = perm_ref[...]
    back = back_ref[...]
    pbias = vec_ref[4:5]
    gain = vec_ref[5:6]
    beta = vec_ref[6:7]
    dbias = vec_ref[7:8]
    for image in range(pics):
        stage_rows(stage, own_ref, recv_ref, image)
        flag = used[step * pics + image].astype(f32)
        rows = pl.ds(image * PIC, PIC)
        cts[rows] = (to_windows(stage, perm, image) * flag).astype(bf16)
    proj = (nn(att_ref[...], wo[...]) + pbias).astype(bf16)
    resid = xw_ref[...].astype(f32) + proj.astype(f32)
    hat, rstd = stats(resid)
    n2s[...] = (hat * gain + beta).astype(bf16)
    mlps[...] = resid + dbias
    gn2s[...] = jnp.zeros_like(gn2s)
    n2t = n2s[...].T
    ctt = cts[...].T
    span = w1.shape[1] // 4

    def chunk(index, carry):
        cols = pl.ds(pl.multiple_of(index * span, span), span)
        pre = nn(n2s[...], w1[:, cols]) + upb_ref[0:1, cols]
        dact = nt(cts[...], w2[cols, :])
        phi = 0.5 * (1.0 + lax.erf(pre * 0.7071067811865476))
        act = (pre * phi).astype(bf16)
        slope = phi + pre * jnp.exp(-0.5 * pre * pre) * 0.3989422804014327
        gpre = dact * slope
        upg_ref[0:1, cols] += rowsum(gpre)
        hidden = gpre.astype(bf16)
        mlps[...] += nn(act, w2[cols, :])
        gn2s[...] += nt(hidden, w1[:, cols])
        acc2[:, cols] += nn(ctt, act)
        acc1[:, cols] += nn(n2t, hidden)
        return carry

    lax.fori_loop(0, 4, chunk, 0)

    gn2 = gn2s[...]
    ct = cts[...].astype(f32)
    gresid = ct + norm_back(gn2 * gain, hat, rstd)
    vecg_ref[4:5] += rowsum(gresid)
    vecg_ref[5:6] += rowsum(gn2 * hat)
    vecg_ref[6:7] += rowsum(gn2)
    vecg_ref[7:8] += rowsum(ct)
    low = gresid.astype(bf16)
    resid_ref[...] = low
    datt = nt(low, wo[...])
    for window in range(2 * pics):
        datt_ref[window, :PAD] = datt[window * PAD : (window + 1) * PAD].astype(bf16)
        datt_ref[window, PAD:] = jnp.zeros((SEG - PAD, D), bf16)
    acco[...] += tn(att_ref[...], low)
    for image in range(pics):
        flag = used[step * pics + image].astype(f32)
        rows = pl.ds(image * PIC, PIC)
        mine = (mlps[rows] * flag).astype(bf16)
        framed = nn(back, mine).astype(bf16).reshape(WIN, COLS, D)
        for row in range(OWN):
            keep_ref[image, row] = framed[row, :SIDE]
        for row in range(SHIFT):
            send_ref[image, row] = framed[OWN + row, :SIDE]

    @pl.when(step == last)
    def _():
        count = D // shards
        tall = w2.shape[0] // shards

        def each(pair, carry):
            for target, flip in ((gkeep_ref, 0), (gsend_ref, 1)):
                place = 2 * pair + ((owners[0] & 1) ^ flip)
                rows = pl.ds(pl.multiple_of(place * count, count), count)
                for piece in range(4):
                    target[pair, piece * count : (piece + 1) * count] = acc1[
                        rows, piece * span : (piece + 1) * span
                    ].astype(bf16)
                cols = pl.ds(pl.multiple_of(place * tall, tall), tall)
                target[pair, 4 * count : 4 * count + tall] = acc2[:, cols].T.astype(bf16)
                target[pair, 4 * count + tall :] = acco[rows].astype(bf16)
            return carry

        lax.fori_loop(0, shards // 2, each, 0)


def backward_attention(
    qkv_ref, datt_ref, table_ref, *rest, pics, chained
):
    dqkv_ref, sum_ref, tab_ref = rest[3 if chained else 0 :]

    @pl.when(pl.program_id(0) == 0)
    def _():
        if chained:
            sum_ref[...] = rest[0][...]
            tab_ref[...] = rest[1][...]
        else:
            sum_ref[...] = jnp.zeros_like(sum_ref)
            tab_ref[...] = jnp.zeros_like(tab_ref)

    masks = head_masks(bf16)
    picks = head_masks(f32)
    units = 2 * GROUPS

    def fold(values):
        return jnp.sum(values.reshape(PAD // 8, 8, LANES), 0)

    def image_step(image, carry):
        state = [None] * units

        def begin(unit):
            window, group = divmod(unit, GROUPS)
            at = group * LANES
            place = image * 2 + window
            query = qkv_ref[place, :, at : at + LANES]
            key = qkv_ref[place, :, D + at : D + at + LANES]
            value = qkv_ref[place, :, 2 * D + at : 2 * D + at + LANES]
            queries = spread(query, masks)
            datts = spread(datt_ref[place, :, at : at + LANES], masks)
            state[unit] = (nt(key, queries)[:PAD], nt(value, datts)[:PAD])

        def soften(unit):
            window, group = divmod(unit, GROUPS)
            raw, dprobs = state[unit]
            scores = raw + table_ref[window, group]
            shifted = jnp.exp(scores - jnp.max(scores, 0, keepdims=True))
            probs = shifted * (1.0 / jnp.sum(shifted, 0, keepdims=True))
            inner = jnp.sum(probs * dprobs, 0, keepdims=True)
            dscores = probs * (dprobs - inner)
            tab_ref[group] += dscores
            state[unit] = (pad_rows(dscores).astype(bf16), pad_rows(probs).astype(bf16))

        def mix(unit):
            window, group = divmod(unit, GROUPS)
            at = group * LANES
            place = image * 2 + window
            dlow, plow = state[unit]
            query = qkv_ref[place, :, at : at + LANES]
            key = qkv_ref[place, :, D + at : D + at + LANES]
            dkey = nn(dlow, spread(query, masks))[:PAD]
            dvalue = nn(plow, spread(datt_ref[place, :, at : at + LANES], masks))[:PAD]
            state[unit] = (dkey, dvalue, tn(dlow, key))

        def finish(unit):
            window, group = divmod(unit, GROUPS)
            at = group * LANES
            dkey, dvalue, tall = state[unit]
            dquery = tall[0:PAD] * picks[0][:PAD]
            for head in range(1, QUAD):
                dquery += tall[head * SEG : head * SEG + PAD] * picks[head][:PAD]
            dquery = dquery * SCALE
            rows = pl.ds(pl.multiple_of(image * PIC + window * PAD, 8), PAD)
            dqkv_ref[rows, at : at + LANES] = dquery.astype(bf16)
            dqkv_ref[rows, D + at : D + at + LANES] = dkey.astype(bf16)
            dqkv_ref[rows, 2 * D + at : 2 * D + at + LANES] = dvalue.astype(bf16)
            sum_ref[0, :, at : at + LANES] += fold(dquery)
            sum_ref[1, :, at : at + LANES] += fold(dvalue)
            state[unit] = None

        begin(0)
        begin(1)
        for unit in range(units):
            soften(unit)
            mix(unit)
            if unit + 2 < units:
                begin(unit + 2)
            if unit > 0:
                finish(unit - 1)
        finish(units - 1)
        return carry

    lax.fori_loop(0, pics, image_step, 0)


def weight_grad(owners, xw_ref, dqkv_ref, vec_ref, gkeep_ref, gsend_ref, acc, *, shards):
    @pl.when(pl.program_id(0) == 0)
    def _():
        clear(acc)

    hat, _ = stats(xw_ref[...].astype(f32))
    normed = (hat * vec_ref[0:1] + vec_ref[1:2]).astype(bf16)
    acc[...] += tn(normed, dqkv_ref[...])

    @pl.when(pl.program_id(0) == pl.num_programs(0) - 1)
    def _():
        count = D // shards
        for pair in range(shards // 2):
            for target, flip in ((gkeep_ref, 0), (gsend_ref, 1)):
                place = 2 * pair + ((owners[0] & 1) ^ flip)
                rows = pl.ds(pl.multiple_of(place * count, count), count)
                target[pair] = acc[rows].astype(bf16)


def input_grad(
    owners, xw_ref, dqkv_ref, resid_ref, back_ref, vec_ref, *rest, shards, pics, chained
):
    weight_refs = rest[:shards]
    keep_ref, send_ref, vecg_ref, weight, sems = rest[shards + (2 if chained else 0) :]

    @pl.when(pl.program_id(0) == 0)
    def _():
        copies = load_shards(owners, weight_refs, weight, sems)
        for copy in copies:
            copy.start()
        vecg_ref[...] = rest[shards][...] if chained else jnp.zeros_like(vecg_ref)
        for copy in copies:
            copy.wait()

    gain = vec_ref[0:1]
    back = back_ref[...]
    hat, rstd = stats(xw_ref[...].astype(f32))
    gnormed = nt(dqkv_ref[...], weight[...]).astype(bf16).astype(f32)
    vecg_ref[0:1] += rowsum(gnormed * hat)
    vecg_ref[1:2] += rowsum(gnormed)
    ginput = resid_ref[...].astype(f32) + norm_back(gnormed * gain, hat, rstd)
    glow = ginput.astype(bf16)
    for image in range(pics):
        framed = nn(back, glow[image * PIC : (image + 1) * PIC]).astype(bf16).reshape(WIN, COLS, D)
        for row in range(OWN):
            keep_ref[image, row] = framed[row, :SIDE]
        for row in range(SHIFT):
            send_ref[image, row] = framed[OWN + row, :SIDE]


def pack_small(*refs, count, span):
    rows_ref = refs[-1]
    up_ref = refs[-2]
    rows_ref[...] = jnp.zeros_like(rows_ref)
    for at in range(count):
        rows_ref[at : at + 1, : refs[at].shape[1]] = refs[at][...].astype(f32)
    for piece in range(up_ref.shape[1] // span):
        at = count + piece
        rows_ref[at : at + 1] = up_ref[:, piece * span : (piece + 1) * span].astype(f32)


def unpack_small(owners, mask_ref, *refs, shards, per, span):
    packs, parts = refs[:shards], refs[shards : 2 * shards]
    vec_ref, up_ref, table_ref, bias = refs[2 * shards :]
    heads = parts[0].shape[1]
    ups = up_ref.shape[1] // shards
    for at in range(shards):
        owner = owners[at]
        vec_ref[:, pl.ds(pl.multiple_of(owner * per, per), per)] = packs[at][:8, :per]
        for piece in range(ups // span):
            cols = pl.ds(pl.multiple_of(owner * ups + piece * span, span), span)
            up_ref[:, cols] = packs[at][8 + piece : 9 + piece]
        bias[:, pl.ds(owner * heads, heads)] = parts[at][...].astype(f32)

    def each(side, carry):
        for group in range(GROUPS):
            wide = jnp.concatenate([bias[side, group * QUAD + head] for head in range(QUAD)], axis=1)
            for window in range(2):
                mask = jnp.concatenate([mask_ref[side, window]] * QUAD, axis=1)
                table_ref[side, window, group] = wide + mask
        return carry

    lax.fori_loop(0, 2, each, 0)


def tie(value, *others):
    return lax.optimization_barrier((value, *others))[0]


class Reduction:
    def __init__(self, keep, send):
        self.keep = keep
        self.send = send
        self.exchange("fsdp", 0)
        img = list(range(bits_of("img")))
        self.plan = (
            [("pick", "fsdp", bit) for bit in range(1, bits_of("fsdp"))]
            + [("halve", "img", bit) for bit in img]
            + [("full", "band", bit) for bit in range(bits_of("band"))]
            + [("join", "img", bit) for bit in reversed(img)]
        )
        self.joined = None

    def total(self, choose=lambda part: part):
        if self.joined is None:
            return (choose(self.keep).astype(f32) + choose(self.got).astype(f32)).astype(bf16)
        first = jnp.concatenate([self.keep, self.got], axis=0)
        second = jnp.concatenate([self.got, self.keep], axis=0)
        return jnp.where(self.joined == 0, first, second)

    def advance(self):
        kind, axis, bit = self.plan.pop(0)
        mine = (lax.axis_index(axis) >> bit) & 1
        if kind in ("pick", "halve"):
            count = self.keep.shape[0]

            def choose(part, at):
                if kind == "pick":
                    pairs = part.reshape(count // 2, 2, *part.shape[1:])
                    return lax.dynamic_index_in_dim(pairs, at, 1, keepdims=False)
                part = part.reshape(2, part.shape[-2] // 2, part.shape[-1])
                return lax.dynamic_index_in_dim(part, at, 0, keepdims=False)

            self.send = self.total(lambda part: choose(part, 1 - mine))
            self.keep = self.total(lambda part: choose(part, mine))
        else:
            self.keep = self.send = self.total()
            self.joined = mine if kind == "join" else None
        self.exchange(axis, bit)
        return self.send

    def exchange(self, axis, bit):
        self.got = partner(self.send, axis, bit)

    def settle(self, value):
        self.got = tie(self.got, value)
        return self.total()[0]

    def advance_after(self, value):
        self.got = tie(self.got, value)
        return self.advance()

    def finish(self):
        while self.plan:
            self.advance()
        return self.total()


def gather(piece):
    held = [piece]
    for bit in reversed(range(bits_of("fsdp"))):
        held = held + [partner(one, "fsdp", bit) for one in held]
    return held


def held_masks():
    masks = [0]
    for bit in reversed(range(bits_of("fsdp"))):
        masks = masks + [mask | (1 << bit) for mask in masks]
    return masks


def window_tables(after=None):
    rows, cols = np.arange(PAD)[:, None], np.arange(SEG)[None, :]
    real = (rows < LEN) & (cols < LEN)

    def index(one, other):
        at = (one // WIN - other // WIN + WIN - 1) * (2 * WIN - 1) + one % WIN - other % WIN + WIN - 1
        return np.where(real, at, TABLE)

    places = jnp.asarray(np.stack([index(rows, cols), index(cols, rows)]), jnp.int32)
    places = lax.optimization_barrier((places, after))[0]
    hots = places[..., None] == jnp.arange(TABLE)
    cells = np.arange(SIDE)
    region = np.where(cells < SIDE - WIN, 0, np.where(cells < SIDE - SHIFT, 1, 2))
    split = region.reshape(SIDE // WIN, WIN)
    label = (split[:, None, :, None] * 3 + split[None, :, None, :]).reshape(2, 2, LEN)
    wide = np.pad(label, ((0, 0), (0, 0), (0, SEG - LEN)), constant_values=-1)
    differ = wide[..., :PAD, None] != wide[..., None, :]
    forward = differ | (cols >= LEN)
    backward = (differ & (cols < LEN)) | (rows >= LEN)
    blocks = np.where(np.stack([forward, backward]), NEGATIVE, 0.0)
    return hots.astype(bf16), jnp.asarray(blocks, f32)


def block_pass(
    block_input,
    slot_used,
    cotangent,
    ln1_gain,
    ln1_bias,
    w_qkv,
    q_bias,
    v_bias,
    rel_table,
    w_out,
    out_bias,
    ln2_gain,
    ln2_bias,
    w_fc1,
    fc1_bias,
    w_fc2,
    fc2_bias,
):
    slots = block_input.shape[0]
    ranks = lax.axis_size("fsdp")
    width = w_fc1.shape[1]
    me = lax.axis_index("fsdp")
    band = lax.axis_index("band")
    owners = jnp.stack([me ^ mask for mask in held_masks()]).astype(jnp.int32)
    cuts = (0, slots // 12 * 10, slots)
    total = slots * PIC

    table_shape = (2, GROUPS, PAD, QUAD * SEG)
    any_spec = pl.BlockSpec(memory_space=pl.ANY)

    def whole(shape):
        return pl.BlockSpec(shape, lambda i, *_: (0,) * len(shape))

    def side(at):
        return pl.BlockSpec((None, *table_shape), lambda i, *_: (at, 0, 0, 0, 0))

    def block(shape, base=0):
        return pl.BlockSpec(shape, lambda i, *_: (i + base,) + (0,) * (len(shape) - 1))

    def like(shape, dtype):
        return jax.ShapeDtypeStruct(shape, dtype)

    params = pltpu.CompilerParams(
        dimension_semantics=("arbitrary",), vmem_limit_bytes=60 * 1024 * 1024
    )

    def call(kernel, micros, grid, prefetch, in_specs, out_specs, out_shape, scratch, aliases={}):
        cost = pl.CostEstimate(
            flops=int(micros * MICRO_FLOPS), bytes_accessed=int(micros * MICRO_BYTES), transcendentals=0
        )
        return pl.pallas_call(
            kernel,
            grid_spec=pltpu.PrefetchScalarGridSpec(
                num_scalar_prefetch=prefetch,
                grid=(grid,),
                in_specs=in_specs,
                out_specs=out_specs,
                scratch_shapes=scratch,
            ),
            out_shape=out_shape,
            input_output_aliases=aliases,
            compiler_params=params,
            cost_estimate=cost,
        )

    arrivals = []
    for piece in range(2):
        edge = block_input[cuts[piece] : cuts[piece + 1], :SHIFT]
        arrivals.append(partner(edge, "band", 0))
    held_qkv = gather(w_qkv)

    per = ln1_gain.shape[0]
    ups = fc1_bias.shape[0]
    heads = rel_table.shape[0]
    span = 2 * LANES
    vectors8 = (ln1_gain, ln1_bias, q_bias, v_bias, out_bias, ln2_gain, ln2_bias, fc2_bias)
    lines = -(-(8 + ups // span) // 8) * 8
    packed = pl.pallas_call(
        functools.partial(pack_small, count=8, span=span),
        out_shape=like((lines, span), f32),
        name="pack_small",
    )(*[one.reshape(1, -1) for one in vectors8], fc1_bias.reshape(1, -1))
    held_small = gather(packed)
    hots, blocks = window_tables()
    local = jnp.einsum("ht,zijt->zhij", rel_table, hots, preferred_element_type=f32)
    held_bias = gather(local.astype(bf16))
    masks = lax.dynamic_index_in_dim(blocks, band, 1, keepdims=False)
    vectors, up_bias, tables = call(
        functools.partial(unpack_small, shards=ranks, per=per, span=span),
        1.0,
        1,
        1,
        [whole((2, 2, PAD, SEG))] + [whole((lines, span))] * ranks
        + [whole((2, heads, PAD, SEG))] * ranks,
        [whole((8, D)), whole((1, width)), whole((2, *table_shape))],
        [like((8, D), f32), like((1, width), f32), like((2, *table_shape), f32)],
        [pltpu.VMEM((2, HEADS, PAD, SEG), f32)],
    )(owners, masks, *held_small, *held_bias)

    target = np.arange(PIC)
    window, spot_in = target // PAD, target % PAD
    source = (spot_in // WIN) * COLS + (window * WIN + spot_in % WIN + SHIFT) % SIDE
    source = np.where(spot_in < LEN, source, -1)
    perm = jnp.asarray(source[:, None] == np.arange(WIN * COLS)[None, :], bf16)
    back = jnp.asarray(source[None, :] == np.arange(WIN * COLS)[:, None], bf16)

    first = lax.optimization_barrier((w_out, w_fc1, w_fc2, held_qkv[-1], held_small[-1], held_bias[-1]))[:3]
    held_late = [[one] for one in first]
    far = bits_of("fsdp") - 1
    for held in held_late:
        held.append(partner(held[0], "fsdp", far))

    ct_arrived = partner(cotangent[:, :SHIFT], "band", 0)

    pics = 4
    rows = pics * PIC
    state = None
    for piece in range(2):
        steps = (cuts[piece + 1] - cuts[piece]) // pics
        base = cuts[piece] // pics
        if piece == 1:
            sends = [held[-1] for held in held_late]
            tied = lax.optimization_barrier((arrivals[piece], state[0], *sends))
            arrivals[piece] = tied[0]
            for held, sent in zip(held_late, tied[2:]):
                held[-1] = sent
                for bit in reversed(range(far)):
                    held.extend([partner(part, "fsdp", bit) for part in held])
        chained = state is not None
        state = call(
            functools.partial(forward_attention, shards=ranks, pics=pics, chained=chained),
            1.6 * (cuts[piece + 1] - cuts[piece]),
            steps,
            1,
            [
                block((pics, WIN, SIDE, D), base), block((pics, SHIFT, SIDE, D)), whole((PIC, PIC)),
                whole((8, D)), side(0),
            ] + [any_spec] * (ranks + (3 if chained else 0)),
            [block((rows, D), base), block((2 * pics, SEG, 3 * D), base), block((rows, D), base)],
            [like((total, D), bf16), like((2 * slots, SEG, 3 * D), bf16), like((total, D), bf16)],
            [
                pltpu.VMEM((D, 3 * D), bf16),
                pltpu.VMEM((pics, WIN, COLS, D), bf16),
                pltpu.VMEM((rows, D), bf16),
                pltpu.SemaphoreType.DMA((ranks,)),
            ],
            {6 + ranks + at: at for at in range(3)} if chained else {},
        )(
            owners, block_input, arrivals[piece], perm, vectors, tables, *held_qkv,
            *(state if chained else ()),
        )
    xw, qkv, att = state
    cotangent = tie(cotangent, ct_arrived)
    held_out, held_up, held_down = held_late

    pack = D // ranks * (width // D) + width // ranks + D // ranks
    half = ranks // 2
    keep, send, resid, datt, gkeep, gsend, vecg, upg = call(
        functools.partial(middle, shards=ranks, pics=pics),
        2.7 * slots,
        slots // pics,
        2,
        [
            block((pics, WIN, SIDE, D)), block((pics, SHIFT, SIDE, D)), block((rows, D)), block((rows, D)),
            whole((PIC, PIC)), whole((PIC, PIC)), whole((8, D)), whole((1, width)),
        ] + [any_spec] * (3 * ranks),
        [
            block((pics, OWN, SIDE, D)), block((pics, SHIFT, SIDE, D)), block((rows, D)),
            block((2 * pics, SEG, D)), whole((half, pack, D)), whole((half, pack, D)),
            whole((8, D)), whole((1, width)),
        ],
        [
            like((slots, OWN, SIDE, D), bf16), like((slots, SHIFT, SIDE, D), bf16),
            like((total, D), bf16), like((2 * slots, SEG, D), bf16), like((half, pack, D), bf16),
            like((half, pack, D), bf16), like((8, D), f32), like((1, width), f32),
        ],
        [
            pltpu.VMEM((D, D), bf16),
            pltpu.VMEM((D, width), bf16),
            pltpu.VMEM((width, D), bf16),
            pltpu.VMEM((pics, WIN, COLS, D), bf16),
            pltpu.VMEM((rows, D), bf16),
            pltpu.VMEM((rows, D), bf16),
            pltpu.VMEM((rows, D), f32),
            pltpu.VMEM((rows, D), f32),
            pltpu.VMEM((D, width), f32),
            pltpu.VMEM((D, width), f32),
            pltpu.VMEM((D, D), f32),
            pltpu.SemaphoreType.DMA((3, ranks)),
        ],
    )(
        owners, slot_used.reshape(-1), cotangent, ct_arrived, xw, att, perm, back, vectors, up_bias,
        *held_out, *held_up, *held_down,
    )

    mlp = Reduction(gkeep, gsend)
    returned = partner(send, "band", 0)
    pics = 2
    rows = pics * PIC
    steps = slots // pics
    first = max(steps // 12, 1)
    early = steps * 7 // 12 * pics
    mid = early // pics + (steps - early // pics + 1) // 2
    sums = tab = lnsum = dqkv = gin = None
    gparts = []

    def attend_part(base, count, tab, sums, dqkv, token):
        chained = dqkv is not None
        if token is not None:
            sums = tie(sums, token)
        return call(
            functools.partial(backward_attention, pics=pics, chained=chained),
            1.9 * 2 * count,
            count,
            0,
            [
                block((2 * pics, SEG, 3 * D), base), block((2 * pics, SEG, D), base),
                side(1),
            ] + [whole((2, 8, D)), whole((GROUPS, PAD, QUAD * SEG)), any_spec] * chained,
            [block((rows, 3 * D), base), whole((2, 8, D)), whole((GROUPS, PAD, QUAD * SEG))],
            [
                like((total, 3 * D), bf16), like((2, 8, D), f32),
                like((GROUPS, PAD, QUAD * SEG), f32),
            ],
            [],
            {5: 0} if chained else {},
        )(qkv, datt, tables, *((sums, tab, dqkv) if chained else ()))

    def descend_part(first, count, lnsum, gin, token):
        images = 4
        tall = images * PIC
        base = first // images
        chained = gin is not None
        if token is not None:
            lnsum = tie(lnsum, token)
        return call(
            functools.partial(input_grad, shards=ranks, pics=images, chained=chained),
            0.8 * count,
            count // images,
            1,
            [
                block((tall, D), base), block((tall, 3 * D), base), block((tall, D), base),
                whole((PIC, PIC)), whole((8, D)),
            ] + [any_spec] * ranks + [whole((8, D)), any_spec] * chained,
            [block((images, OWN, SIDE, D), base), block((images, SHIFT, SIDE, D)), whole((8, D))],
            [
                like((slots, OWN, SIDE, D), bf16), like((count, SHIFT, SIDE, D), bf16),
                like((8, D), f32),
            ],
            [
                pltpu.VMEM((D, 3 * D), bf16),
                pltpu.SemaphoreType.DMA((ranks,)),
            ],
            {7 + ranks: 0} if chained else {},
        )(
            owners, xw, dqkv, resid, back, vectors, *held_qkv, *((lnsum, gin) if chained else ()),
        )

    dqkv, sums, tab = attend_part(0, first, tab, sums, dqkv, None)
    token = mlp.advance_after(sums)
    dqkv, sums, tab = attend_part(first, early // pics - first, tab, sums, dqkv, token)
    token = mlp.advance_after(sums)
    dqkv, sums, tab = attend_part(early // pics, mid - early // pics, tab, sums, dqkv, token)
    token = mlp.advance_after(sums)
    dqkv, sums, tab = attend_part(mid, steps - mid, tab, sums, dqkv, token)
    token = mlp.advance_after(sums)

    images = 4
    tall = images * PIC
    qkeep, qsend = call(
        functools.partial(weight_grad, shards=ranks),
        0.49 * slots,
        slots // images,
        1,
        [block((tall, D)), block((tall, 3 * D)), whole((8, D))],
        [whole((half, D // ranks, 3 * D)), whole((half, D // ranks, 3 * D))],
        [like((half, D // ranks, 3 * D), bf16), like((half, D // ranks, 3 * D), bf16)],
        [pltpu.VMEM((D, 3 * D), f32)],
    )(owners, xw, dqkv, tie(vectors, token))
    token = mlp.advance_after(qkeep)
    own = Reduction(qkeep, qsend)
    gin, gpart, lnsum = descend_part(0, slots, lnsum, gin, token)
    gparts.append(partner(gpart, "band", 0))
    mlp.advance_after(lnsum)

    count = D // ranks
    lanes = width // D
    spots, sums, two = lax.optimization_barrier((tab, sums, window_tables(lnsum)[0][1]))[:3]
    spots = spots.reshape(GROUPS, PAD, QUAD, SEG)
    grad_table = jnp.einsum(
        "gihj,ijt->ght", spots.astype(bf16), two, preferred_element_type=f32
    )
    flat = jnp.concatenate([
        lnsum[:2], jnp.sum(sums, 1), vecg[4:], upg.reshape(-1, D),
        jnp.pad(grad_table.reshape(HEADS, TABLE), ((0, 0), (0, D - TABLE))),
    ])
    own.advance()
    swaps = [(axis, bit) for axis in ("fsdp", "img", "band") for bit in range(bits_of(axis))]
    while own.plan or swaps:
        token = own.got
        if swaps:
            got = partner(flat, *swaps.pop(0))
            flat, token = lax.optimization_barrier((flat + got, token))
        own.got = token
        if own.plan:
            own.advance()
    mine = lax.dynamic_index_in_dim(flat[:8].reshape(8, ranks, per), me, 1, keepdims=False)
    own_upb = lax.dynamic_slice_in_dim(flat[8 : 8 + lanes].reshape(-1), me * ups, ups)
    own_table = lax.dynamic_slice_in_dim(flat, 8 + lanes + me * heads, heads)[:, :TABLE]
    packed = mlp.finish().astype(f32)
    own_up = packed[: lanes * count].reshape(lanes, count, D).transpose(1, 0, 2).reshape(count, width)
    own_down = packed[lanes * count : lanes * count + width // ranks]
    own_out = packed[lanes * count + width // ranks :]

    own_qkv = own.finish().astype(f32)

    def lead(part):
        return jnp.transpose(part, (1, 2, 0, 3))

    output = jnp.concatenate([returned, keep], axis=1)
    halo = jnp.concatenate([lead(part) for part in gparts], axis=2)
    grad_input = jnp.transpose(
        jnp.concatenate([halo, lead(gin)], axis=0).astype(f32), (2, 0, 1, 3)
    )
    return (
        output,
        grad_input,
        mine[0],
        mine[1],
        own_qkv,
        mine[2],
        mine[3],
        own_table,
        own_out,
        mine[4],
        mine[5],
        mine[6],
        own_up,
        own_upb,
        own_down,
        mine[7],
    )


def solution(mesh):
    pictures = P(("img", "fsdp"), "band", None, None)
    flat = P("fsdp")
    wide = P("fsdp", None)
    return jax.shard_map(
        block_pass,
        mesh=mesh,
        in_specs=(
            pictures, P(("img", "fsdp"), None), pictures, flat, flat, wide, flat, flat, wide, wide,
            flat, flat, flat, wide, flat, wide, flat,
        ),
        out_specs=(
            pictures, pictures, flat, flat, wide, flat, flat, wide, wide, flat, flat, flat, wide,
            flat, wide, flat,
        ),
        check_vma=False,
    )
```
